1024 devices in a mesh: seq: 128 (over y_hi, z, x), mp: 4 (over y_lo), role: 2 (over core).
Axes of the slice: x: 8, y: 8 (y_hi: 2, y_lo: 4; y = y_hi * 4 + y_lo), z: 8, core: 2. Of those that a mesh axis runs over, the one named last changes fastest.
Arguments:
- gen_hidden: bfloat16 [128, 256, 3072], P('seq', None, ('mp', 'role')), may hold values from -6 to 6
- gen_out_weight: bfloat16 [3072, 128], P(('mp', 'role')), may hold values from -0.109375 to 0.109375
- patch_order: int32 [128], replicated, may hold values from 0 to 127, each once
- frame_block: int32 [256], replicated, may hold values from 0 to 128, as said below
- embed_weight: bfloat16 [128, 3072], replicated, may hold values from -0.5 to 0.5
- pos_table: bfloat16 [128, 3072], replicated, may hold values from -3 to 3
- norm_gain: bfloat16 [3072], replicated, may hold values from 0.099609375 to 1.8984375
- qkv_weight: bfloat16 [3072, 3, 2048], P(None, None, ('mp', 'role')), may hold values from -0.109375 to 0.109375
- out_weight: bfloat16 [2048, 3072], P(('mp', 'role')), may hold values from -0.125 to 0.125
Outputs:
- disc_out: bfloat16 [32768, 3072], P(('seq', 'mp', 'role'))
The draws below stay inside these ranges and needn't reach their ends.
Inputs may be any that keep to these rules, and one draw needn't show every extreme that they name: `patch_order`: each patch position appears in exactly one slot. `frame_block`: blocks are runs of consecutive frames with indices never falling, each of 1 to 4 frames, at least one of exactly 4; frames share a block iff their indices are equal.
All inputs are finite; a program needn't handle non-finite values.
Results may differ from the reference program's by a relative error of at most 0.006.
Values may be sent and summed in bfloat16 or wider, within the bound.
A program may use at most 64 MiB of HBM per device.

```python
import jax
import jax.numpy as jnp
from jax import lax

D = 3072
HEADS = 16
HS = 128
P_SIZE = 128
MOSTB = 4
PATCHES = 128
FRAMES = 256
TOKENS = 32768


def draw_frame_block(key, part):
    frame = jnp.arange(FRAMES, dtype=jnp.int32)
    pairs = (frame + 1) // 2
    quads = pairs // 2
    second = pairs % 2
    merged = jax.random.randint(jax.random.fold_in(key, 7), (FRAMES // 4 + 2,), 0, 2, dtype=jnp.int32)
    merged = merged.at[1].set(1)
    merged = merged.at[FRAMES // 4].set(0)
    joined = merged[quads]
    return (2 * quads + second * (1 - joined)).astype(jnp.int32)


def steps_of(key, shape, cuts, least, top_value):
    factor_of = 1.0
    for axis_at, blocks in cuts:
        draws = jax.random.uniform(jax.random.fold_in(jax.random.fold_in(key, 6), axis_at), (blocks,), jnp.float32, least / len(cuts), top_value / len(cuts))
        factor_of = factor_of * jnp.repeat(jnp.exp(draws), shape[axis_at] // blocks).reshape((-1,) + (1,) * (len(shape) - 1 - axis_at))
    return factor_of


def noise(key, shape, spread, bound, split=(), kind=jnp.bfloat16):
    loudness = steps_of(key, shape, split, -0.22, 0.18) if split else 1.0
    drawn = jax.random.normal(key, shape, jnp.float32) * spread * loudness
    return jnp.minimum(jnp.maximum(drawn, -bound), bound).astype(kind)


def setup_inputs(seed: int = 0) -> dict:
    splits = jax.random.split(jax.random.key(seed), 10)
    return {
        "gen_hidden": noise(splits[0], (PATCHES, FRAMES, D), 1.0, 6.0, ((0, 128), (2, 8))),
        "gen_out_weight": noise(splits[1], (D, P_SIZE), D ** -0.5, 0.109375, ((0, 8),)),
        "patch_order": jax.random.permutation(splits[2], PATCHES).astype(jnp.int32),
        "frame_block": draw_frame_block(jax.random.fold_in(splits[9], 71), 0),
        "embed_weight": noise(splits[4], (P_SIZE, D), P_SIZE ** -0.5, 0.5),
        "pos_table": noise(splits[5], (PATCHES, D), 0.5, 3.0),
        "norm_gain": jnp.clip(1.0 + 0.18 * jax.random.normal(splits[6], (D,), jnp.float32), 0.099609375, 1.8984375).astype(jnp.bfloat16),
        "qkv_weight": noise(splits[7], (D, 3, HEADS * HS), D ** -0.5, 0.109375, ((2, 8),)),
        "out_weight": noise(splits[8], (HEADS * HS, D), (HEADS * HS) ** -0.5, 0.125, ((0, 8),)),
    }


def frame_attention(query, keys, values, mask, head_size):
    tq = query.shape[0]
    scores = jnp.einsum('qhe,khe->hqk', query.astype(jnp.float32), keys.astype(jnp.float32)) / jnp.sqrt(jnp.float32(head_size))
    scores = jnp.where(mask[None], scores, jnp.float32(-1e+30))
    top = lax.optimization_barrier(jnp.max(scores, axis=-1, keepdims=True))
    expo = jnp.where(mask[None], jnp.exp(scores - top), jnp.float32(0.0))
    probs = (expo / lax.optimization_barrier(jnp.sum(expo, axis=-1, keepdims=True))).astype(jnp.bfloat16)
    mixed = jnp.einsum('hqk,khe->qhe', probs.astype(jnp.float32), values.astype(jnp.float32))
    return mixed.astype(jnp.bfloat16).reshape(tq, -1)

def reference(gen_hidden, gen_out_weight, patch_order, frame_block, embed_weight, pos_table, norm_gain, qkv_weight, out_weight):
    slot_latents = jnp.dot(gen_hidden.reshape(-1, D), gen_out_weight, preferred_element_type=jnp.float32)
    slot_latents = slot_latents.astype(jnp.bfloat16).reshape(PATCHES, FRAMES, P_SIZE)
    inverse = jnp.zeros((PATCHES,), jnp.int32).at[patch_order].set(jnp.arange(PATCHES, dtype=jnp.int32))
    latents = jnp.transpose(slot_latents[inverse], (1, 0, 2))
    embedded = jnp.dot(latents.reshape(-1, P_SIZE), embed_weight, preferred_element_type=jnp.float32).reshape(FRAMES, PATCHES, D)
    embedded = embedded + pos_table.astype(jnp.float32)[None]
    scale = lax.rsqrt(lax.optimization_barrier(jnp.mean(embedded * embedded, axis=-1, keepdims=True)) + 1e-06)
    normed = (embedded * scale * norm_gain.astype(jnp.float32)).astype(jnp.bfloat16)
    proj = jnp.dot(normed.reshape(-1, D), qkv_weight.reshape(D, 3 * HEADS * HS), preferred_element_type=jnp.float32)
    proj = proj.astype(jnp.bfloat16).reshape(FRAMES, PATCHES, 3, HEADS, HS)
    query = proj[:, :, 0]
    reach = MOSTB - 1
    width = 2 * reach + 1
    keys = jnp.pad(proj[:, :, 1], ((reach, reach), (0, 0), (0, 0), (0, 0)))
    values = jnp.pad(proj[:, :, 2], ((reach, reach), (0, 0), (0, 0), (0, 0)))
    blocks = jnp.pad(frame_block, (reach, reach), constant_values=-1)

    def one_frame(frame):
        start = frame.astype(jnp.int32)
        near_k = lax.dynamic_slice_in_dim(keys, start, width, 0).reshape(width * PATCHES, HEADS, HS)
        near_v = lax.dynamic_slice_in_dim(values, start, width, 0).reshape(width * PATCHES, HEADS, HS)
        near_b = lax.dynamic_slice_in_dim(blocks, start, width, 0)
        own_b = lax.dynamic_slice_in_dim(frame_block, start, 1, 0)
        frame_mask = jnp.repeat(near_b == own_b, PATCHES)
        mask = jnp.broadcast_to(frame_mask[None, :], (PATCHES, width * PATCHES))
        own_q = lax.dynamic_slice_in_dim(query, start, 1, 0)[0]
        return frame_attention(own_q, near_k, near_v, mask, HS)
    attn = lax.map(one_frame, jnp.arange(FRAMES, dtype=jnp.int32)).reshape(TOKENS, HEADS * HS)
    mixed = jnp.dot(attn, out_weight, preferred_element_type=jnp.float32)
    return (embedded.reshape(TOKENS, D) + mixed).astype(jnp.bfloat16)
```

```python
import functools

import jax
import jax.numpy as jnp
from jax import lax
from jax.experimental import pallas as pl
from jax.experimental.pallas import tpu as pltpu
from jax.sharding import PartitionSpec as P

MESH = pl.DeviceIdType.MESH
F32 = jnp.float32
BF16 = jnp.bfloat16
HS = 128
CHUNKS = 4
NEG = -1e30


def dot(a, b, precision=None):
    return jnp.dot(a, b, preferred_element_type=F32, precision=precision)


def dot_t(a, b, precision=None):
    return lax.dot_general(
        a, b, (((1,), (1,)), ((), ())), preferred_element_type=F32, precision=precision
    )


def split2(a):
    hi = a.astype(BF16)
    return hi, (a - hi.astype(F32)).astype(BF16)


def iota(shape, dim):
    return lax.broadcasted_iota(jnp.int32, shape, dim)


def kernel(
    gh_hbm,
    gw_hbm,
    po_ref,
    fb_ref,
    e_hbm,
    pos_hbm,
    gain_ref,
    w_hbm,
    wo_hbm,
    out_ref,
    gh,
    gw,
    e,
    pos,
    w,
    wo,
    ppad,
    send_a,
    recv_a,
    send_x,
    recv_x,
    send_z,
    lat,
    kv,
    fhl,
    m_all,
    fv_all,
    sel_q,
    hr2,
    he2,
    ncol,
    nlane,
    bias,
    gg,
    lat_q,
    q_all,
    u_all,
    a_all,
    acc,
    send_c,
    recv_c,
    load_sem,
    sa,
    ra,
    sx,
    rx,
    sz,
    rz,
    sf,
    rf,
    sp,
    rp,
    sc,
    rc,
):
    seq = lax.axis_index("seq")
    m = lax.axis_index("mp")
    r = lax.axis_index("role")
    ys = seq // 64
    z = (seq // 8) % 8
    x = seq % 8
    j = 2 * m + r
    y = ys * 4 + m
    is_self = jnp.logical_and(j == z, True)

    def group(k):
        return (seq, k // 2, k % 2)

    def row_x(x2):
        return (ys * 64 + z * 8 + x2, m, r)

    def ring(y2, role):
        return ((y2 // 4) * 64 + z * 8 + x, y2 % 4, role)

    def zy_source(idx):
        return ((idx // 4) * 64 + (2 * (idx % 4) + r) * 8 + x, z // 2, z % 2)

    def zy_dest(i):
        y2 = (y + i) % 8
        return ((y2 // 4) * 64 + j * 8 + x, y2 % 4, z % 2)

    partner = (seq, m, 1 - r)

    barrier = pltpu.get_barrier_semaphore()

    def greet(device):
        pl.semaphore_signal(barrier, inc=1, device_id=device, device_id_type=MESH)

    for step in range(1, 8):
        greet(group((j + step) % 8))
        greet(row_x((x + step) % 8))
    for idx in range(8):
        here = jnp.logical_and(is_self, idx == ys * 4 + z // 2)

        @pl.when(jnp.logical_not(here))
        def _():
            greet(zy_source(idx))

    for step in range(1, 4):
        i = (1 + r + step) % 4
        greet(ring((y + 1 + r - i + 8) % 8, r))

    def load(src, dst, n):
        return pltpu.make_async_copy(src, dst, load_sem.at[n])

    loads = [
        load(gh_hbm, gh, 0),
        load(gw_hbm, gw, 1),
        load(e_hbm, e, 2),
        load(pos_hbm, pos, 3),
        load(w_hbm, w, 4),
        load(wo_hbm, wo.at[r], 5),
    ]
    for copy in loads:
        copy.start()

    ppad[0:8, :] = jnp.zeros((8, 128), F32)
    ppad[264:288, :] = jnp.zeros((24, 128), F32)

    po_f = jnp.broadcast_to(po_ref[...], (16, 128)).astype(F32).astype(BF16)
    spread = (iota((128, 1024), 0) == lax.shift_right_logical(iota((128, 1024), 1), 3)).astype(
        F32
    ).astype(BF16)
    po_lane = dot(po_f, spread)[0:1]
    perm_t = (jnp.broadcast_to(po_ref[...], (128, 128)) == iota((128, 128), 0)).astype(F32).astype(
        BF16
    )
    rows8 = (lax.shift_right_logical(iota((1024, 128), 0), 3) == iota((1024, 128), 1)).astype(
        F32
    ).astype(BF16)
    onehot = dot_t(rows8, perm_t).astype(BF16)
    kv[0, :, 128:256] = onehot
    kv[1, :, 128:256] = onehot
    w_lane = jnp.bitwise_and(iota((1, 1024), 1), 7)
    for yt in range(2):
        base = yt * 128 + z * 16 + x * 2 - 3
        blocks = []
        key_block = jnp.full((1, 1024), -1, jnp.int32)
        for n in range(8):
            frame = base + n
            value = fb_ref[jnp.clip(frame, 0, 255)]
            value = jnp.where(jnp.logical_and(frame >= 0, frame <= 255), value, -1)
            blocks.append(value)
            key_block = jnp.where(w_lane == n, value, key_block)
        for fi in range(2):
            bias[yt, fi] = jnp.where(key_block == blocks[3 + fi], F32(0), F32(NEG))
    for i in range(4):
        d = (y - 1 - r + i + 8) % 8
        fi = (d % 4) // 2
        patch = ((d % 2) * 2 + r) * 32
        rows = (iota((32, 1024), 0) + patch).astype(F32)
        hit = jnp.logical_and(
            jnp.broadcast_to(po_lane, (32, 1024)) == rows,
            jnp.broadcast_to(w_lane, (32, 1024)) == 3 + fi,
        )
        sel_q[i] = hit.astype(F32).astype(BF16)

    loads[0].wait()
    loads[1].wait()
    ppad[8:264, :] = dot(gh[...], gw[...])
    for k in range(8):
        for yt in range(2):
            first = 128 * yt + 16 * k + 5
            send_a[k, 24 * yt : 24 * yt + 24, :] = ppad[first : first + 24, :]

    pl.semaphore_wait(barrier, 25 - is_self.astype(jnp.int32))

    def copy_a(step):
        k = (j + step) % 8
        return pltpu.make_async_remote_copy(
            send_a.at[k], recv_a.at[j], sa.at[step], ra.at[j], group(k), MESH
        )

    def land_a(step):
        k = (j + step) % 8
        return pltpu.make_async_remote_copy(
            send_a.at[k], recv_a.at[k], sa.at[step], ra.at[k], group(k), MESH
        )

    for step in range(1, 8):
        copy_a(step).start()
    loads[5].wait()
    wo_copy = pltpu.make_async_remote_copy(
        wo.at[r], wo.at[r], sp.at[0], rp.at[0], partner, MESH
    )
    wo_copy.start()

    loads[2].wait()
    loads[3].wait()
    gain = gain_ref[...].astype(F32)
    for n, table in enumerate((e, pos)):
        hi, lo = split2(table[...].astype(F32) * gain)
        fhl[n * 128 : n * 128 + 128, :] = hi
        fhl[256 + n * 128 : 384 + n * 128, :] = lo
    ghi, glo = split2(dot_t(e[...], e[...]))
    gg[:, 0:128] = ghi
    gg[:, 128:256] = glo
    he = 2.0 * dot_t(pos[...], e[...])
    he2[...] = he
    he_hi, he_lo = split2(he)
    hr2[...] = dot(onehot, he_hi) + dot(onehot, he_lo)
    norms = dot_t(pos[...], pos[...])
    diagonal = jnp.where(iota((128, 128), 0) == iota((128, 128), 1), norms, F32(0))
    ncol[...] = jnp.broadcast_to(jnp.sum(diagonal, axis=1, keepdims=True), (128, 128))
    nrow = jnp.broadcast_to(jnp.sum(diagonal, axis=0, keepdims=True), (8, 128))
    nlane[...] = dot_t(nrow, onehot.astype(F32), lax.Precision.HIGHEST)[0:1]
    loads[4].wait()

    def weight_product(c):
        both = dot(fhl[...], w[c])
        return both[0:256] + both[256:512]

    for step in range(1, 8):
        land_a(step).wait_recv()
    total = send_a[j]
    for step in range(1, 8):
        total = total + recv_a[(j + step) % 8]
    recv_a[j] = total
    for n in range(8):
        halves = [recv_a[j, 24 * yt + 2 * n : 24 * yt + 2 * n + 8, :] for yt in range(2)]
        send_x[n] = jnp.concatenate(halves, axis=0).astype(BF16)

    def copy_x(step):
        x2 = (x + step) % 8
        return pltpu.make_async_remote_copy(
            send_x.at[x2], recv_x.at[x], sx.at[step], rx.at[x], row_x(x2), MESH
        )

    def land_x(step):
        x2 = (x + step) % 8
        return pltpu.make_async_remote_copy(
            send_x.at[x2], recv_x.at[x2], sx.at[step], rx.at[x2], row_x(x2), MESH
        )

    for step in range(1, 8):
        copy_x(step).start()
    recv_x[x] = send_x[x]

    fq = weight_product(0)
    fk = weight_product(1)

    for step in range(1, 8):
        land_x(step).wait_recv()
    for a in range(4):
        first = recv_x[2 * a].astype(F32)
        second = recv_x[2 * a + 1].astype(F32)
        for yt in range(2):
            pair = jnp.concatenate(
                [first[8 * yt : 8 * yt + 8], second[8 * yt : 8 * yt + 8]], axis=0
            )
            send_z[yt, 16 * a : 16 * a + 16, :] = pair.astype(BF16)

    own_block = ys * 8 + z
    own_idx = ys * 4 + z // 2

    def copy_z(i):
        return pltpu.make_async_remote_copy(
            send_z, lat.at[:, own_block], sz.at[i], rz.at[own_idx], zy_dest(i), MESH
        )

    local_z = pltpu.make_async_copy(send_z, lat.at[:, own_block], rz.at[own_idx])
    for i in range(1, 8):
        copy_z(i).start()

    @pl.when(jnp.logical_not(is_self))
    def _():
        copy_z(0).start()

    @pl.when(is_self)
    def _():
        local_z.start()

    for h in range(2):
        cols = slice(HS * h, HS * h + HS)
        bil = dot_t(fq[:, cols], fk[:, cols], lax.Precision.HIGHEST)
        hi, lo = split2(bil)
        m_all[r, 0, :, 256 * h : 256 * h + 256] = hi
        m_all[r, 1, :, 256 * h : 256 * h + 256] = lo
    hi, lo = split2(weight_product(2))
    fv_all[r, 0] = hi
    fv_all[r, 1] = lo
    m_copy = pltpu.make_async_remote_copy(
        m_all.at[r], m_all.at[r], sp.at[1], rp.at[1], partner, MESH
    )
    f_copy = pltpu.make_async_remote_copy(
        fv_all.at[r], fv_all.at[r], sp.at[2], rp.at[2], partner, MESH
    )
    m_copy.start()
    f_copy.start()

    def block_of(idx, role):
        return (idx // 4) * 8 + 2 * (idx % 4) + role

    def forward(idx):
        b = block_of(idx, r)
        return pltpu.make_async_remote_copy(
            lat.at[:, b], lat.at[:, b], sf.at[idx], rf.at[idx], partner, MESH
        )

    def forwarded(idx):
        b = block_of(idx, 1 - r)
        return pltpu.make_async_remote_copy(
            lat.at[:, b], lat.at[:, b], sf.at[idx], rf.at[idx], partner, MESH
        )

    for idx in range(8):
        b = block_of(idx, r)
        pltpu.make_async_copy(lat.at[:, b], lat.at[:, b], rz.at[idx]).wait()
        forward(idx).start()
    for idx in range(8):
        forwarded(idx).wait_recv()

    scale_k = []
    ones = jnp.ones((8, 128), F32)
    for yt in range(2):
        rows = lat[yt].reshape(1024, 128)
        kv[yt, :, 0:128] = rows
        both = dot(rows, gg[...])
        z_part = rows.astype(F32) * (both[:, 0:128] + both[:, 128:256] + hr2[...])
        total = dot_t(ones, z_part, lax.Precision.HIGHEST)[0:1] + nlane[...]
        scale_k.append(lax.rsqrt(jnp.maximum(total, 0.0) * F32(1 / 3072) + F32(1e-06)))
    for yt in range(2):
        bias[yt, 2] = scale_k[yt]

    tokens = []
    scales = []
    for i in range(4):
        d = (y - 1 - r + i + 8) % 8
        patch = pl.multiple_of(((d % 2) * 2 + r) * 32, 32)
        mine = dot(sel_q[i], kv[d // 4, :, 0:128])
        lat_q[32 * i : 32 * i + 32, :] = mine.astype(BF16)
        both = dot(mine.astype(BF16), gg[...])
        squares = mine * (both[:, 0:128] + both[:, 128:256] + he2[pl.ds(patch, 32), :])
        total = jnp.sum(squares, axis=1, keepdims=True) + ncol[pl.ds(patch, 32), 0:1]
        scales.append(
            lax.rsqrt(jnp.maximum(total, 0.0) * F32(1 / 3072) + F32(1e-06))
            * F32(1 / HS**0.5)
        )
        place = (iota((32, 128), 0) + patch == iota((32, 128), 1)).astype(F32).astype(BF16)
        tokens.append(jnp.concatenate([mine.astype(BF16), place], axis=1))
    tokens = jnp.concatenate(tokens, axis=0)
    scales = jnp.concatenate(scales, axis=0)
    pltpu.make_async_remote_copy(
        m_all.at[1 - r], m_all.at[1 - r], sp.at[1], rp.at[1], partner, MESH
    ).wait_recv()
    for role in range(2):
        q = (dot(tokens, m_all[role, 0]) + dot(tokens, m_all[role, 1])) * scales
        for h in range(2):
            q_all[2 * role + h] = q[:, 256 * h : 256 * h + 256].astype(BF16)

    for i in range(4):
        d = (y - 1 - r + i + 8) % 8
        yt = d // 4
        fi = (d % 4) // 2
        keys = kv[yt]
        q = q_all[:, 32 * i : 32 * i + 32, :].reshape(128, 256)
        scale = bias[yt, 2]
        s = dot_t(q, keys) * scale + bias[yt, fi]
        top = jnp.max(s, axis=1, keepdims=True)
        expo = jnp.exp(s - top)
        norm = jnp.sum(expo, axis=1, keepdims=True)
        u = dot((expo * scale).astype(BF16), keys) / norm
        u_all[:, 32 * i : 32 * i + 32, :] = u.reshape(4, 32, 256)

    pltpu.make_async_remote_copy(
        fv_all.at[1 - r], fv_all.at[1 - r], sp.at[2], rp.at[2], partner, MESH
    ).wait_recv()
    for role in range(2):
        for h in range(2):
            hi, lo = split2(u_all[2 * role + h])
            cols = slice(HS * h, HS * h + HS)
            v_hi = fv_all[role, 0, :, cols]
            v_lo = fv_all[role, 1, :, cols]
            a = dot(hi, v_hi) + dot(lo, v_hi) + dot(hi, v_lo)
            a_all[:, 256 * role + HS * h : 256 * role + HS * h + HS] = a.astype(BF16)

    pltpu.make_async_remote_copy(
        wo.at[1 - r], wo.at[1 - r], sp.at[0], rp.at[0], partner, MESH
    ).wait_recv()
    width = 3072 // CHUNKS
    own_i = 1 + r

    def copy_c(c, step):
        i = (own_i + step) % 4
        d = (y - 1 - r + i + 8) % 8
        return pltpu.make_async_remote_copy(
            send_c.at[c, i], recv_c.at[c, i], sc.at[c, step], rc.at[c, i], ring(d, r), MESH
        )

    def land_c(c, step):
        i = (own_i + step) % 4
        d = (y + 1 + r - i + 8) % 8
        return pltpu.make_async_remote_copy(
            send_c.at[c, i], recv_c.at[c, i], sc.at[c, step], rc.at[c, i], ring(d, r), MESH
        )

    for c in range(CHUNKS):
        cols = slice(width * c, width * c + width)
        part = dot(a_all[:, 0:256], wo[0, :, cols]) + dot(a_all[:, 256:512], wo[1, :, cols])
        part = part.reshape(4, 32, width)
        acc[c] = part
        send_c[c] = part.astype(BF16)
        for step in range(1, 4):
            copy_c(c, step).start()

    own_lat = lat_q[pl.ds(pl.multiple_of(own_i * 32, 32), 32), :]
    own_patch = pl.multiple_of(((m % 2) * 2 + r) * 32, 32)
    for c in range(CHUNKS):
        cols = slice(width * c, width * c + width)
        embedded = dot(own_lat, e[:, cols]) + pos[pl.ds(own_patch, 32), cols].astype(F32)
        acc[c, own_i] = acc[c, own_i] + embedded
    for c in range(CHUNKS):
        cols = slice(width * c, width * c + width)
        total = acc[c, own_i]
        for step in range(1, 4):
            land_c(c, step).wait_recv()
            total = total + recv_c[c, (own_i + step) % 4].astype(F32)
        out_ref[:, cols] = total.astype(BF16)

    for step in range(1, 8):
        copy_a(step).wait_send()
        copy_x(step).wait_send()
        copy_z(step).wait_send()

    @pl.when(jnp.logical_not(is_self))
    def _():
        copy_z(0).wait_send()

    for idx in range(8):
        forward(idx).wait_send()
    wo_copy.wait_send()
    m_copy.wait_send()
    f_copy.wait_send()
    for c in range(CHUNKS):
        for step in range(1, 4):
            copy_c(c, step).wait_send()


def on_device(
    gen_hidden,
    gen_out_weight,
    patch_order,
    frame_block,
    embed_weight,
    pos_table,
    norm_gain,
    qkv_weight,
    out_weight,
):
    any_space = pl.BlockSpec(memory_space=pl.ANY)
    vmem = pl.BlockSpec(memory_space=pltpu.VMEM)
    smem = pl.BlockSpec(memory_space=pltpu.SMEM)
    dma = pltpu.SemaphoreType.DMA
    width = 3072 // CHUNKS
    scratch = [
        pltpu.VMEM((256, 384), BF16),
        pltpu.VMEM((384, 128), BF16),
        pltpu.VMEM((128, 3072), BF16),
        pltpu.VMEM((128, 3072), BF16),
        pltpu.VMEM((3, 3072, 256), BF16),
        pltpu.VMEM((2, 256, 3072), BF16),
        pltpu.VMEM((288, 128), F32),
        pltpu.VMEM((8, 48, 128), F32),
        pltpu.VMEM((8, 48, 128), F32),
        pltpu.VMEM((8, 16, 128), BF16),
        pltpu.VMEM((8, 16, 128), BF16),
        pltpu.VMEM((2, 64, 128), BF16),
        pltpu.VMEM((2, 16, 64, 128), BF16),
        pltpu.VMEM((2, 1024, 256), BF16),
        pltpu.VMEM((512, 3072), BF16),
        pltpu.VMEM((2, 2, 256, 512), BF16),
        pltpu.VMEM((2, 2, 256, 256), BF16),
        pltpu.VMEM((4, 32, 1024), BF16),
        pltpu.VMEM((1024, 128), F32),
        pltpu.VMEM((128, 128), F32),
        pltpu.VMEM((128, 128), F32),
        pltpu.VMEM((1, 1024), F32),
        pltpu.VMEM((2, 3, 1, 1024), F32),
        pltpu.VMEM((128, 256), BF16),
        pltpu.VMEM((128, 128), BF16),
        pltpu.VMEM((4, 128, 256), BF16),
        pltpu.VMEM((4, 128, 256), F32),
        pltpu.VMEM((128, 512), BF16),
        pltpu.VMEM((CHUNKS, 4, 32, width), F32),
        pltpu.VMEM((CHUNKS, 4, 32, width), BF16),
        pltpu.VMEM((CHUNKS, 4, 32, width), BF16),
        dma((6,)),
        dma((8,)),
        dma((8,)),
        dma((8,)),
        dma((8,)),
        dma((8,)),
        dma((8,)),
        dma((8,)),
        dma((8,)),
        dma((3,)),
        dma((3,)),
        dma((CHUNKS, 4)),
        dma((CHUNKS, 4)),
    ]
    return pl.pallas_call(
        kernel,
        out_shape=jax.ShapeDtypeStruct((32, 3072), BF16),
        in_specs=[
            any_space,
            any_space,
            vmem,
            smem,
            any_space,
            any_space,
            vmem,
            any_space,
            any_space,
        ],
        out_specs=vmem,
        scratch_shapes=scratch,
        compiler_params=pltpu.CompilerParams(collective_id=0, has_side_effects=True),
    )(
        gen_hidden.reshape(256, 384),
        gen_out_weight,
        patch_order.reshape(1, 128),
        frame_block,
        embed_weight,
        pos_table,
        norm_gain.reshape(1, 3072),
        jnp.transpose(qkv_weight, (1, 0, 2)),
        out_weight,
    )


def solution(mesh):
    in_specs = (
        P("seq", None, ("mp", "role")),
        P(("mp", "role"), None),
        P(),
        P(),
        P(),
        P(),
        P(),
        P(None, None, ("mp", "role")),
        P(("mp", "role"), None),
    )
    out_specs = P(("seq", "mp", "role"), None)
    return jax.shard_map(
        on_device, mesh=mesh, in_specs=in_specs, out_specs=out_specs, check_vma=False
    )
```

```python
import functools

import jax
import jax.numpy as jnp
from jax import lax
from jax.experimental import pallas as pl
from jax.experimental.pallas import tpu as pltpu
from jax.sharding import PartitionSpec as P

MESH = pl.DeviceIdType.MESH
F32 = jnp.float32
BF16 = jnp.bfloat16
HS = 128
CHUNKS = 4
NEG = -1e30


def dot(a, b, precision=None):
    return jnp.dot(a, b, preferred_element_type=F32, precision=precision)


def dot_t(a, b, precision=None):
    return lax.dot_general(
        a, b, (((1,), (1,)), ((), ())), preferred_element_type=F32, precision=precision
    )


def split2(a):
    hi = a.astype(BF16)
    return hi, (a - hi.astype(F32)).astype(BF16)


def iota(shape, dim):
    return lax.broadcasted_iota(jnp.int32, shape, dim)


def slot_of(row):
    part = lax.shift_right_logical(row, 3)
    parity = lax.shift_right_logical(part, 6)
    half = jnp.bitwise_and(lax.shift_right_logical(part, 5), 1)
    rest = jnp.bitwise_and(lax.shift_right_logical(part, 3), 3)
    return half * 64 + rest * 16 + parity * 8 + jnp.bitwise_and(part, 7)


def kernel(
    gh_hbm,
    gw_hbm,
    po_hbm,
    fb_hbm,
    e_hbm,
    pos_hbm,
    gain_hbm,
    w_hbm,
    wo_hbm,
    out_hbm,
    gh,
    gw,
    po_ref,
    fb_ref,
    gain_ref,
    out_ref,
    e,
    pos,
    w,
    wo,
    ppad,
    send_a,
    recv_a,
    send_x,
    recv_x,
    send_z,
    lat,
    kv,
    fhl,
    m_all,
    fv_all,
    sel_q,
    hr2,
    he2,
    ncol,
    nlane,
    bias,
    key_scale,
    gg,
    lat_q,
    q_all,
    u_all,
    a_all,
    acc,
    send_c,
    recv_c,
    load_sem,
    out_sem,
    sa,
    ra,
    sx,
    rx,
    sz,
    rz,
    sf,
    rf,
    sp,
    rp,
    sc,
    rc,
):
    seq = lax.axis_index("seq")
    m = lax.axis_index("mp")
    r = lax.axis_index("role")
    ys = seq // 64
    z = (seq // 8) % 8
    x = seq % 8
    j = 2 * m + r
    y = ys * 4 + m
    is_self = jnp.logical_and(j == z, True)

    def group(k):
        return (seq, k // 2, k % 2)

    def row_x(x2):
        return (ys * 64 + z * 8 + x2, m, r)

    def ring(y2, role):
        return ((y2 // 4) * 64 + z * 8 + x, y2 % 4, role)

    def zy_source(idx):
        return ((idx // 4) * 64 + (2 * (idx % 4) + r) * 8 + x, z // 2, z % 2)

    def zy_dest(i):
        y2 = (y + i) % 8
        return ((y2 // 4) * 64 + j * 8 + x, y2 % 4, z % 2)

    def place_of(p):
        first = 2 * (1 - r) if p < 2 else 2 * r
        return (y - 1 - r + first + p % 2 + 8) % 8

    def source_of(p):
        first = 2 * (1 - r) if p < 2 else 2 * r
        return (y + 1 + r - first - p % 2 + 8) % 8

    partner = (seq, m, 1 - r)

    def load(src, dst, n):
        return pltpu.make_async_copy(src, dst, load_sem.at[n])

    load_gh = load(gh_hbm, gh, 0)
    load_gw = load(gw_hbm, gw, 1)
    load_po = load(po_hbm, po_ref, 2)
    load_fb = load(fb_hbm, fb_ref, 3)
    load_gain = load(gain_hbm, gain_ref, 4)
    load_e = load(e_hbm, e, 5)
    load_pos = load(pos_hbm, pos, 6)
    load_w = load(w_hbm, w, 7)
    load_wo = load(wo_hbm, wo.at[r], 8)
    for copy in (load_gh, load_gw, load_po, load_fb, load_gain):
        copy.start()

    barrier = pltpu.get_barrier_semaphore()

    def greet(device):
        pl.semaphore_signal(barrier, inc=1, device_id=device, device_id_type=MESH)

    for step in range(1, 8):
        greet(group((j + step) % 8))
        greet(row_x((x + step) % 8))
    for idx in range(8):
        here = jnp.logical_and(is_self, idx == ys * 4 + z // 2)

        @pl.when(jnp.logical_not(here))
        def _():
            greet(zy_source(idx))

    for step in range(1, 4):
        i = (1 + r + step) % 4
        greet(ring((y + 1 + r - i + 8) % 8, r))

    ppad[0:8, :] = jnp.zeros((8, 128), F32)
    ppad[264:288, :] = jnp.zeros((24, 128), F32)

    load_gh.wait()
    load_gw.wait()
    ppad[8:264, :] = dot(gh[...], gw[...])
    for k in range(8):
        for yt in range(2):
            first = 128 * yt + 16 * k + 5
            send_a[k, 24 * yt : 24 * yt + 24, :] = ppad[first : first + 24, :]

    pl.semaphore_wait(barrier, 25 - is_self.astype(jnp.int32))

    def copy_a(step):
        k = (j + step) % 8
        return pltpu.make_async_remote_copy(
            send_a.at[k], recv_a.at[j], sa.at[step], ra.at[j], group(k), MESH
        )

    def land_a(step):
        k = (j + step) % 8
        return pltpu.make_async_remote_copy(
            send_a.at[k], recv_a.at[k], sa.at[step], ra.at[k], group(k), MESH
        )

    for step in range(1, 8):
        copy_a(step).start()
    for copy in (load_e, load_pos, load_w, load_wo):
        copy.start()

    load_po.wait()
    load_fb.wait()
    po_f = jnp.broadcast_to(po_ref[...], (16, 128)).astype(F32).astype(BF16)
    spread = (iota((128, 1024), 0) == slot_of(iota((128, 1024), 1))).astype(F32).astype(BF16)
    po_lane = dot(po_f, spread)[0:1]
    perm_t = (jnp.broadcast_to(po_ref[...], (128, 128)) == iota((128, 128), 0)).astype(F32).astype(
        BF16
    )
    rows8 = (slot_of(iota((1024, 128), 0)) == iota((1024, 128), 1)).astype(F32).astype(BF16)
    onehot = dot_t(rows8, perm_t).astype(BF16)
    kv[0, :, 128:256] = onehot
    kv[1, :, 128:256] = onehot
    w_lane = jnp.bitwise_and(iota((1, 1024), 1), 7)
    for yt in range(2):
        base = yt * 128 + z * 16 + x * 2 - 3
        blocks = []
        key_block = jnp.full((1, 1024), -1, jnp.int32)
        for n in range(8):
            frame = base + n
            value = fb_ref[jnp.clip(frame, 0, 255)]
            value = jnp.where(jnp.logical_and(frame >= 0, frame <= 255), value, -1)
            blocks.append(value)
            key_block = jnp.where(w_lane == n, value, key_block)
        for fi in range(2):
            bias[yt, fi] = jnp.where(key_block == blocks[3 + fi], F32(0), F32(NEG))
    for p in range(4):
        d = place_of(p)
        fi = (d % 4) // 2
        patch = ((d % 2) * 2 + r) * 32
        rows = (iota((32, 1024), 0) + patch).astype(F32)
        hit = jnp.logical_and(
            jnp.broadcast_to(po_lane, (32, 1024)) == rows,
            jnp.broadcast_to(w_lane, (32, 1024)) == 3 + fi,
        )
        sel_q[p] = hit.astype(F32).astype(BF16)

    load_e.wait()
    load_pos.wait()
    load_gain.wait()
    gain = gain_ref[...].astype(F32)
    for n, table in enumerate((e, pos)):
        for part in range(24):
            cols = slice(128 * part, 128 * part + 128)
            hi, lo = split2(table[:, cols].astype(F32) * gain[part : part + 1, :])
            fhl[n * 128 : n * 128 + 128, cols] = hi
            fhl[256 + n * 128 : 384 + n * 128, cols] = lo
    ghi, glo = split2(dot_t(e[...], e[...]))
    gg[:, 0:128] = ghi
    gg[:, 128:256] = glo
    he = 2.0 * dot_t(pos[...], e[...])
    he2[...] = he
    he_hi, he_lo = split2(he)
    hr2[...] = dot(onehot, he_hi) + dot(onehot, he_lo)
    norms = dot_t(pos[...], pos[...])
    diagonal = jnp.where(iota((128, 128), 0) == iota((128, 128), 1), norms, F32(0))
    ncol[...] = jnp.broadcast_to(jnp.sum(diagonal, axis=1, keepdims=True), (128, 128))
    nrow = jnp.broadcast_to(jnp.sum(diagonal, axis=0, keepdims=True), (8, 128))
    norm_lane = dot_t(nrow, onehot.astype(F32), lax.Precision.HIGHEST)[0:1]
    for n in range(4):
        nlane[n] = norm_lane[:, 256 * n : 256 * n + 256]
    load_w.wait()
    load_wo.wait()
    wo_copy = pltpu.make_async_remote_copy(
        wo.at[r], wo.at[r], sp.at[0], rp.at[0], partner, MESH
    )
    wo_copy.start()

    def weight_product(c):
        both = dot(fhl[...], w[c])
        return both[0:256] + both[256:512]

    for step in range(1, 8):
        land_a(step).wait_recv()
    total = send_a[j]
    for step in range(1, 8):
        total = total + recv_a[(j + step) % 8]
    recv_a[j] = total
    for n in range(8):
        halves = [recv_a[j, 24 * yt + 2 * n : 24 * yt + 2 * n + 8, :] for yt in range(2)]
        send_x[n] = jnp.concatenate(halves, axis=0).astype(BF16)

    def copy_x(step):
        x2 = (x + step) % 8
        return pltpu.make_async_remote_copy(
            send_x.at[x2], recv_x.at[x], sx.at[step], rx.at[x], row_x(x2), MESH
        )

    def land_x(step):
        x2 = (x + step) % 8
        return pltpu.make_async_remote_copy(
            send_x.at[x2], recv_x.at[x2], sx.at[step], rx.at[x2], row_x(x2), MESH
        )

    for step in range(1, 8):
        copy_x(step).start()
    recv_x[x] = send_x[x]

    fq = weight_product(0)
    fk = weight_product(1)

    for step in range(1, 8):
        land_x(step).wait_recv()
    for a in range(4):
        first = recv_x[2 * a].astype(F32)
        second = recv_x[2 * a + 1].astype(F32)
        for yt in range(2):
            pair = jnp.concatenate(
                [first[8 * yt : 8 * yt + 8], second[8 * yt : 8 * yt + 8]], axis=0
            )
            send_z[yt, 16 * a : 16 * a + 16, :] = pair.astype(BF16)

    half = z % 2
    own_idx = ys * 4 + z // 2

    def copy_z(i):
        return pltpu.make_async_remote_copy(
            send_z, lat.at[:, half, own_idx], sz.at[i], rz.at[own_idx], zy_dest(i), MESH
        )

    local_z = pltpu.make_async_copy(send_z, lat.at[:, half, own_idx], rz.at[own_idx])
    for i in range(1, 8):
        copy_z(i).start()

    @pl.when(jnp.logical_not(is_self))
    def _():
        copy_z(0).start()

    @pl.when(is_self)
    def _():
        local_z.start()

    for h in range(2):
        cols = slice(HS * h, HS * h + HS)
        bil = dot_t(fq[:, cols], fk[:, cols], lax.Precision.HIGHEST)
        hi, lo = split2(bil)
        m_all[r, 0, :, 256 * h : 256 * h + 256] = hi
        m_all[r, 1, :, 256 * h : 256 * h + 256] = lo
    hi, lo = split2(weight_product(2))
    fv_all[r, 0] = hi
    fv_all[r, 1] = lo
    m_copy = pltpu.make_async_remote_copy(
        m_all.at[r], m_all.at[r], sp.at[1], rp.at[1], partner, MESH
    )
    f_copy = pltpu.make_async_remote_copy(
        fv_all.at[r], fv_all.at[r], sp.at[2], rp.at[2], partner, MESH
    )
    m_copy.start()
    f_copy.start()

    def forward(idx):
        block = lat.at[:, r, idx]
        return pltpu.make_async_remote_copy(
            block, block, sf.at[idx], rf.at[idx], partner, MESH
        )

    def forwarded(idx):
        block = lat.at[:, 1 - r, idx]
        return pltpu.make_async_remote_copy(
            block, block, sf.at[idx], rf.at[idx], partner, MESH
        )

    ones = jnp.ones((8, 128), F32)

    def take_batch(parity, n):
        batch = parity * 2 + n
        first = pl.multiple_of(batch * 256, 256)
        for yt in range(2):
            rows = lat[yt, parity, 4 * n : 4 * n + 4].reshape(256, 128)
            kv[yt, pl.ds(first, 256), 0:128] = rows
            both = dot(rows, gg[...])
            cross = both[:, 0:128] + both[:, 128:256] + hr2[pl.ds(first, 256), :]
            total = dot_t(ones, rows.astype(F32) * cross, lax.Precision.HIGHEST)[0:1]
            total = total + nlane[batch]
            key_scale[yt, batch] = lax.rsqrt(
                jnp.maximum(total, 0.0) * F32(1 / 3072) + F32(1e-06)
            )

    for n in range(2):
        for idx in range(4 * n, 4 * n + 4):
            block = lat.at[:, r, idx]
            pltpu.make_async_copy(block, block, rz.at[idx]).wait()
            forward(idx).start()
        take_batch(r, n)
    for n in range(2):
        for idx in range(4 * n, 4 * n + 4):
            forwarded(idx).wait_recv()
        take_batch(1 - r, n)

    tokens = []
    scales = []
    for p in range(4):
        d = place_of(p)
        patch = pl.multiple_of(((d % 2) * 2 + r) * 32, 32)
        mine = dot(sel_q[p], kv[d // 4, :, 0:128])
        lat_q[32 * p : 32 * p + 32, :] = mine.astype(BF16)
        both = dot(mine.astype(BF16), gg[...])
        squares = mine * (both[:, 0:128] + both[:, 128:256] + he2[pl.ds(patch, 32), :])
        total = jnp.sum(squares, axis=1, keepdims=True) + ncol[pl.ds(patch, 32), 0:1]
        scales.append(
            lax.rsqrt(jnp.maximum(total, 0.0) * F32(1 / 3072) + F32(1e-06))
            * F32(1 / HS**0.5)
        )
        place = (iota((32, 128), 0) + patch == iota((32, 128), 1)).astype(F32).astype(BF16)
        tokens.append(jnp.concatenate([mine.astype(BF16), place], axis=1))
    tokens = jnp.concatenate(tokens, axis=0)
    scales = jnp.concatenate(scales, axis=0)
    pltpu.make_async_remote_copy(
        m_all.at[1 - r], m_all.at[1 - r], sp.at[1], rp.at[1], partner, MESH
    ).wait_recv()
    for role in range(2):
        q = (dot(tokens, m_all[role, 0]) + dot(tokens, m_all[role, 1])) * scales
        for h in range(2):
            q_all[2 * role + h] = q[:, 256 * h : 256 * h + 256].astype(BF16)

    width = 3072 // CHUNKS

    def copy_c(c, p):
        return pltpu.make_async_remote_copy(
            send_c.at[c, p], recv_c.at[c, p], sc.at[c, p], rc.at[c, p], ring(place_of(p), r), MESH
        )

    def land_c(c, p):
        return pltpu.make_async_remote_copy(
            send_c.at[c, p], recv_c.at[c, p], sc.at[c, p], rc.at[c, p], ring(source_of(p), r), MESH
        )

    near = 2 + r

    def copy_near(c):
        d = (y + 1 - 2 * (1 - r) + 8) % 8
        return pltpu.make_async_remote_copy(
            send_c.at[c, near],
            recv_c.at[c, near],
            sc.at[c, near],
            rc.at[c, near],
            ring(d, r),
            MESH,
        )

    def land_near(c):
        d = (y - 1 + 2 * (1 - r) + 8) % 8
        return pltpu.make_async_remote_copy(
            send_c.at[c, near],
            recv_c.at[c, near],
            sc.at[c, near],
            rc.at[c, near],
            ring(d, r),
            MESH,
        )

    for g in range(2):
        for p in (2 * g, 2 * g + 1):
            d = place_of(p)
            yt = d // 4
            fi = (d % 4) // 2
            keys = kv[yt]
            q = q_all[:, 32 * p : 32 * p + 32, :].reshape(128, 256)
            scale = jnp.concatenate([key_scale[yt, n] for n in range(4)], axis=1)
            s = dot_t(q, keys) * scale + bias[yt, fi]
            top = jnp.max(s, axis=1, keepdims=True)
            expo = jnp.exp(s - top)
            norm = jnp.sum(expo, axis=1, keepdims=True)
            u = dot((expo * scale).astype(BF16), keys) / norm
            u_all[:, 32 * p : 32 * p + 32, :] = u.reshape(4, 32, 256)
        if g == 0:
            pltpu.make_async_remote_copy(
                fv_all.at[1 - r], fv_all.at[1 - r], sp.at[2], rp.at[2], partner, MESH
            ).wait_recv()
            pltpu.make_async_remote_copy(
                wo.at[1 - r], wo.at[1 - r], sp.at[0], rp.at[0], partner, MESH
            ).wait_recv()
        rows = slice(64 * g, 64 * g + 64)
        for role in range(2):
            for h in range(2):
                hi, lo = split2(u_all[2 * role + h, rows, :])
                cols = slice(HS * h, HS * h + HS)
                v_hi = fv_all[role, 0, :, cols]
                v_lo = fv_all[role, 1, :, cols]
                a = dot(hi, v_hi) + dot(lo, v_hi) + dot(hi, v_lo)
                a_all[rows, 256 * role + HS * h : 256 * role + HS * h + HS] = a.astype(BF16)
        for c in range(CHUNKS):
            cols = slice(width * c, width * c + width)
            part = dot(a_all[rows, 0:256], wo[0, :, cols]) + dot(
                a_all[rows, 256:512], wo[1, :, cols]
            )
            part = part.reshape(2, 32, width)
            send_c[c, 2 * g : 2 * g + 2] = part.astype(BF16)
            if g == 0:
                copy_c(c, 0).start()
                copy_c(c, 1).start()
            else:
                acc[c] = part
                copy_near(c).start()

    own_lat = lat_q[pl.ds(pl.multiple_of((3 - r) * 32, 32), 32), :]
    own_patch = pl.multiple_of(((m % 2) * 2 + r) * 32, 32)
    for c in range(CHUNKS):
        cols = slice(width * c, width * c + width)
        embedded = dot(own_lat, e[:, cols]) + pos[pl.ds(own_patch, 32), cols].astype(F32)
        acc[c, 1 - r] = acc[c, 1 - r] + embedded
    outs = []
    for c in range(CHUNKS):
        cols = slice(width * c, width * c + width)
        land_c(c, 0).wait_recv()
        land_c(c, 1).wait_recv()
        land_near(c).wait_recv()
        total = acc[c, 1 - r] + recv_c[c, 0].astype(F32)
        total = total + recv_c[c, 1].astype(F32)
        total = total + recv_c[c, near].astype(F32)
        out_ref[:, cols] = total.astype(BF16)
        outs.append(
            pltpu.make_async_copy(out_ref.at[:, cols], out_hbm.at[:, cols], out_sem.at[c])
        )
        outs[-1].start()

    for step in range(1, 8):
        copy_a(step).wait_send()
        copy_x(step).wait_send()
        copy_z(step).wait_send()

    @pl.when(jnp.logical_not(is_self))
    def _():
        copy_z(0).wait_send()

    for idx in range(8):
        forward(idx).wait_send()
    wo_copy.wait_send()
    m_copy.wait_send()
    f_copy.wait_send()
    for c in range(CHUNKS):
        copy_c(c, 0).wait_send()
        copy_c(c, 1).wait_send()
        copy_near(c).wait_send()
    for copy in outs:
        copy.wait()


def on_device(
    gen_hidden,
    gen_out_weight,
    patch_order,
    frame_block,
    embed_weight,
    pos_table,
    norm_gain,
    qkv_weight,
    out_weight,
):
    any_space = pl.BlockSpec(memory_space=pl.ANY)
    dma = pltpu.SemaphoreType.DMA
    width = 3072 // CHUNKS
    scratch = [
        pltpu.VMEM((256, 384), BF16),
        pltpu.VMEM((384, 128), BF16),
        pltpu.VMEM((1, 128), jnp.int32),
        pltpu.SMEM((256,), jnp.int32),
        pltpu.VMEM((24, 128), BF16),
        pltpu.VMEM((32, 3072), BF16),
        pltpu.VMEM((128, 3072), BF16),
        pltpu.VMEM((128, 3072), BF16),
        pltpu.VMEM((3, 3072, 256), BF16),
        pltpu.VMEM((2, 256, 3072), BF16),
        pltpu.VMEM((288, 128), F32),
        pltpu.VMEM((8, 48, 128), F32),
        pltpu.VMEM((8, 48, 128), F32),
        pltpu.VMEM((8, 16, 128), BF16),
        pltpu.VMEM((8, 16, 128), BF16),
        pltpu.VMEM((2, 64, 128), BF16),
        pltpu.VMEM((2, 2, 8, 64, 128), BF16),
        pltpu.VMEM((2, 1024, 256), BF16),
        pltpu.VMEM((512, 3072), BF16),
        pltpu.VMEM((2, 2, 256, 512), BF16),
        pltpu.VMEM((2, 2, 256, 256), BF16),
        pltpu.VMEM((4, 32, 1024), BF16),
        pltpu.VMEM((1024, 128), F32),
        pltpu.VMEM((128, 128), F32),
        pltpu.VMEM((128, 128), F32),
        pltpu.VMEM((4, 1, 256), F32),
        pltpu.VMEM((2, 2, 1, 1024), F32),
        pltpu.VMEM((2, 4, 1, 256), F32),
        pltpu.VMEM((128, 256), BF16),
        pltpu.VMEM((128, 128), BF16),
        pltpu.VMEM((4, 128, 256), BF16),
        pltpu.VMEM((4, 128, 256), F32),
        pltpu.VMEM((128, 512), BF16),
        pltpu.VMEM((CHUNKS, 2, 32, width), F32),
        pltpu.VMEM((CHUNKS, 4, 32, width), BF16),
        pltpu.VMEM((CHUNKS, 4, 32, width), BF16),
        dma((9,)),
        dma((CHUNKS,)),
        dma((8,)),
        dma((8,)),
        dma((8,)),
        dma((8,)),
        dma((8,)),
        dma((8,)),
        dma((8,)),
        dma((8,)),
        dma((3,)),
        dma((3,)),
        dma((CHUNKS, 4)),
        dma((CHUNKS, 4)),
    ]
    return pl.pallas_call(
        kernel,
        out_shape=jax.ShapeDtypeStruct((32, 3072), BF16),
        in_specs=[any_space] * 9,
        out_specs=any_space,
        scratch_shapes=scratch,
        compiler_params=pltpu.CompilerParams(collective_id=0, has_side_effects=True),
    )(
        gen_hidden.reshape(256, 384),
        gen_out_weight,
        patch_order.reshape(1, 128),
        frame_block,
        embed_weight,
        pos_table,
        norm_gain.reshape(24, 128),
        jnp.transpose(qkv_weight, (1, 0, 2)),
        out_weight,
    )


def solution(mesh):
    in_specs = (
        P("seq", None, ("mp", "role")),
        P(("mp", "role"), None),
        P(),
        P(),
        P(),
        P(),
        P(),
        P(None, None, ("mp", "role")),
        P(("mp", "role"), None),
    )
    out_specs = P(("seq", "mp", "role"), None)
    return jax.shard_map(
        on_device, mesh=mesh, in_specs=in_specs, out_specs=out_specs, check_vma=False
    )
```

```python
import functools

import jax
import jax.numpy as jnp
from jax import lax
from jax.experimental import pallas as pl
from jax.experimental.pallas import tpu as pltpu
from jax.sharding import PartitionSpec as P

MESH = pl.DeviceIdType.MESH
F32 = jnp.float32
BF16 = jnp.bfloat16
HS = 128
CHUNKS = 4
NEG = -1e30


def dot(a, b, precision=None):
    return jnp.dot(a, b, preferred_element_type=F32, precision=precision)


def dot_t(a, b, precision=None):
    return lax.dot_general(
        a, b, (((1,), (1,)), ((), ())), preferred_element_type=F32, precision=precision
    )


def split2(a):
    hi = a.astype(BF16)
    return hi, (a - hi.astype(F32)).astype(BF16)


def iota(shape, dim):
    return lax.broadcasted_iota(jnp.int32, shape, dim)


def slot_of(row):
    part = lax.shift_right_logical(row, 3)
    parity = lax.shift_right_logical(part, 6)
    half = jnp.bitwise_and(lax.shift_right_logical(part, 5), 1)
    rest = jnp.bitwise_and(lax.shift_right_logical(part, 3), 3)
    return half * 64 + rest * 16 + parity * 8 + jnp.bitwise_and(part, 7)


def kernel(
    gh_hbm,
    gw_hbm,
    po_hbm,
    fb_hbm,
    e_hbm,
    pos_hbm,
    gain_hbm,
    w_hbm,
    wo_hbm,
    out_hbm,
    gh,
    gw,
    po_ref,
    fb_ref,
    gain_ref,
    out_ref,
    e,
    pos,
    w,
    wo,
    ppad,
    mine,
    send_a,
    recv_a,
    send_x,
    recv_x,
    send_z,
    lat,
    kv,
    fhl,
    m_all,
    fv_all,
    sel_q,
    hr2,
    he2,
    ncol,
    nlane,
    bias,
    key_scale,
    gg,
    lat_q,
    q_all,
    u_all,
    a_all,
    acc,
    send_c,
    recv_c,
    load_sem,
    out_sem,
    sa,
    ra,
    sx,
    rx,
    sz,
    rz,
    sf,
    rf,
    sp,
    rp,
    sc,
    rc,
):
    seq = lax.axis_index("seq")
    m = lax.axis_index("mp")
    r = lax.axis_index("role")
    ys = seq // 64
    z = (seq // 8) % 8
    x = seq % 8
    j = 2 * m + r
    y = ys * 4 + m
    is_self = jnp.logical_and(j == z, True)

    def group(k):
        return (seq, k // 2, k % 2)

    def row_x(x2):
        return (ys * 64 + z * 8 + x2, m, r)

    def ring(y2, role):
        return ((y2 // 4) * 64 + z * 8 + x, y2 % 4, role)

    def zy_source(idx):
        return ((idx // 4) * 64 + (2 * (idx % 4) + r) * 8 + x, z // 2, z % 2)

    def zy_dest(i):
        y2 = (y + i) % 8
        return ((y2 // 4) * 64 + j * 8 + x, y2 % 4, z % 2)

    side = 1 - 2 * r
    offsets = (2, -1, 1, 0)

    def place_of(p):
        return (y + side * offsets[p] + 8) % 8

    def source_of(p):
        return (y - side * offsets[p] + 8) % 8

    partner = (seq, m, 1 - r)

    def load(src, dst, n):
        return pltpu.make_async_copy(src, dst, load_sem.at[n])

    load_gh = load(gh_hbm, gh, 0)
    load_gw = load(gw_hbm, gw, 1)
    load_po = load(po_hbm, po_ref, 2)
    load_fb = load(fb_hbm, fb_ref, 3)
    load_gain = load(gain_hbm, gain_ref, 4)
    load_e = load(e_hbm, e, 5)
    load_pos = load(pos_hbm, pos, 6)
    load_w = load(w_hbm, w, 7)
    load_wo = load(wo_hbm, wo.at[r], 8)
    load_gh.start()
    load_gw.start()

    barrier = pltpu.get_barrier_semaphore()

    def greet(device):
        pl.semaphore_signal(barrier, inc=1, device_id=device, device_id_type=MESH)

    for idx in range(8):
        here = jnp.logical_and(is_self, idx == ys * 4 + z // 2)

        @pl.when(jnp.logical_not(here))
        def _():
            greet(zy_source(idx))

    for step in range(1, 8):
        greet(row_x((x + step) % 8))
    for step in range(1, 8):
        greet(group((j + step) % 8))
    for p in range(3):
        greet(ring(source_of(p), r))

    for copy in (load_po, load_fb, load_gain):
        copy.start()
    ppad[0:8, :] = jnp.zeros((8, 128), F32)
    ppad[264:288, :] = jnp.zeros((24, 128), F32)

    load_gh.wait()
    load_gw.wait()
    ppad[8:264, :] = dot(gh[...], gw[...])
    for k in range(8):
        parts = [ppad[128 * yt + 16 * k + 5 : 128 * yt + 16 * k + 29, :] for yt in range(2)]
        part = jnp.concatenate(parts, axis=0)
        mine[k] = part
        send_a[k] = part.astype(BF16)

    pl.semaphore_wait(barrier, 25 - is_self.astype(jnp.int32))

    def copy_a(step):
        k = (j + step) % 8
        return pltpu.make_async_remote_copy(
            send_a.at[k], recv_a.at[j], sa.at[step], ra.at[j], group(k), MESH
        )

    def land_a(step):
        k = (j + step) % 8
        return pltpu.make_async_remote_copy(
            send_a.at[k], recv_a.at[k], sa.at[step], ra.at[k], group(k), MESH
        )

    for step in range(1, 8):
        copy_a(step).start()
    for copy in (load_e, load_pos, load_w, load_wo):
        copy.start()
    wo_copy = pltpu.make_async_remote_copy(
        wo_hbm, wo.at[r], sp.at[0], rp.at[0], partner, MESH
    )
    wo_copy.start()

    load_po.wait()
    load_fb.wait()
    po_f = jnp.broadcast_to(po_ref[...], (16, 128)).astype(F32).astype(BF16)
    spread = (iota((128, 1024), 0) == slot_of(iota((128, 1024), 1))).astype(F32).astype(BF16)
    po_lane = dot(po_f, spread)[0:1]
    perm_t = (jnp.broadcast_to(po_ref[...], (128, 128)) == iota((128, 128), 0)).astype(F32).astype(
        BF16
    )
    rows8 = (slot_of(iota((1024, 128), 0)) == iota((1024, 128), 1)).astype(F32).astype(BF16)
    onehot = dot_t(rows8, perm_t).astype(BF16)
    kv[0, :, 128:256] = onehot
    kv[1, :, 128:256] = onehot
    w_lane = jnp.bitwise_and(iota((1, 1024), 1), 7)
    for yt in range(2):
        base = yt * 128 + z * 16 + x * 2 - 3
        blocks = []
        key_block = jnp.full((1, 1024), -1, jnp.int32)
        for n in range(8):
            frame = base + n
            value = fb_ref[jnp.clip(frame, 0, 255)]
            value = jnp.where(jnp.logical_and(frame >= 0, frame <= 255), value, -1)
            blocks.append(value)
            key_block = jnp.where(w_lane == n, value, key_block)
        for fi in range(2):
            bias[yt, fi] = jnp.where(key_block == blocks[3 + fi], F32(0), F32(NEG))
    for p in range(4):
        d = place_of(p)
        fi = (d % 4) // 2
        patch = ((d % 2) * 2 + r) * 32
        rows = (iota((32, 1024), 0) + patch).astype(F32)
        hit = jnp.logical_and(
            jnp.broadcast_to(po_lane, (32, 1024)) == rows,
            jnp.broadcast_to(w_lane, (32, 1024)) == 3 + fi,
        )
        sel_q[p] = hit.astype(F32).astype(BF16)

    load_e.wait()
    load_pos.wait()
    load_gain.wait()
    gain = gain_ref[...].astype(F32)
    for n, table in enumerate((e, pos)):
        for part in range(24):
            cols = slice(128 * part, 128 * part + 128)
            hi, lo = split2(table[:, cols].astype(F32) * gain[part : part + 1, :])
            fhl[n * 128 : n * 128 + 128, cols] = hi
            fhl[256 + n * 128 : 384 + n * 128, cols] = lo
    ghi, glo = split2(dot_t(e[...], e[...]))
    gg[:, 0:128] = ghi
    gg[:, 128:256] = glo
    he = 2.0 * dot_t(pos[...], e[...])
    he2[...] = he
    he_hi, he_lo = split2(he)
    hr2[...] = dot(onehot, he_hi) + dot(onehot, he_lo)
    norms = dot_t(pos[...], pos[...])
    diagonal = jnp.where(iota((128, 128), 0) == iota((128, 128), 1), norms, F32(0))
    ncol[...] = jnp.broadcast_to(jnp.sum(diagonal, axis=1, keepdims=True), (128, 128))
    nrow = jnp.broadcast_to(jnp.sum(diagonal, axis=0, keepdims=True), (8, 128))
    norm_lane = dot_t(nrow, onehot.astype(F32), lax.Precision.HIGHEST)[0:1]
    for n in range(4):
        nlane[n] = norm_lane[:, 256 * n : 256 * n + 256]
    load_w.wait()
    load_wo.wait()

    def weight_product(c):
        both = dot(fhl[...], w[c])
        return both[0:256] + both[256:512]

    for step in range(1, 8):
        land_a(step).wait_recv()
    total = mine[j]
    for step in range(1, 8):
        total = total + recv_a[(j + step) % 8].astype(F32)
    mine[j] = total
    for n in range(8):
        halves = [mine[j, 24 * yt + 2 * n : 24 * yt + 2 * n + 8, :] for yt in range(2)]
        send_x[n] = jnp.concatenate(halves, axis=0).astype(BF16)

    def copy_x(step):
        x2 = (x + step) % 8
        return pltpu.make_async_remote_copy(
            send_x.at[x2], recv_x.at[x], sx.at[step], rx.at[x], row_x(x2), MESH
        )

    def land_x(step):
        x2 = (x + step) % 8
        return pltpu.make_async_remote_copy(
            send_x.at[x2], recv_x.at[x2], sx.at[step], rx.at[x2], row_x(x2), MESH
        )

    for step in range(1, 8):
        copy_x(step).start()
    recv_x[x] = send_x[x]

    fq = weight_product(0)
    fk = weight_product(1)

    for step in range(1, 8):
        land_x(step).wait_recv()
    for a in range(4):
        first = recv_x[2 * a].astype(F32)
        second = recv_x[2 * a + 1].astype(F32)
        for yt in range(2):
            pair = jnp.concatenate(
                [first[8 * yt : 8 * yt + 8], second[8 * yt : 8 * yt + 8]], axis=0
            )
            send_z[yt, 16 * a : 16 * a + 16, :] = pair.astype(BF16)

    half = z % 2
    own_idx = ys * 4 + z // 2

    def copy_z(i):
        return pltpu.make_async_remote_copy(
            send_z, lat.at[:, half, own_idx], sz.at[i], rz.at[own_idx], zy_dest(i), MESH
        )

    local_z = pltpu.make_async_copy(send_z, lat.at[:, half, own_idx], rz.at[own_idx])
    for i in range(1, 8):
        copy_z(i).start()

    @pl.when(jnp.logical_not(is_self))
    def _():
        copy_z(0).start()

    @pl.when(is_self)
    def _():
        local_z.start()

    for h in range(2):
        cols = slice(HS * h, HS * h + HS)
        bil = dot_t(fq[:, cols], fk[:, cols], lax.Precision.HIGHEST)
        hi, lo = split2(bil)
        m_all[r, 0, :, 256 * h : 256 * h + 256] = hi
        m_all[r, 1, :, 256 * h : 256 * h + 256] = lo
    hi, lo = split2(weight_product(2))
    fv_all[r, 0] = hi
    fv_all[r, 1] = lo
    m_copy = pltpu.make_async_remote_copy(
        m_all.at[r], m_all.at[r], sp.at[1], rp.at[1], partner, MESH
    )
    f_copy = pltpu.make_async_remote_copy(
        fv_all.at[r], fv_all.at[r], sp.at[2], rp.at[2], partner, MESH
    )
    m_copy.start()
    f_copy.start()

    def forward(idx):
        block = lat.at[:, r, idx]
        return pltpu.make_async_remote_copy(
            block, block, sf.at[idx], rf.at[idx], partner, MESH
        )

    def forwarded(idx):
        block = lat.at[:, 1 - r, idx]
        return pltpu.make_async_remote_copy(
            block, block, sf.at[idx], rf.at[idx], partner, MESH
        )

    ones = jnp.ones((8, 128), F32)

    def take_batch(parity, n):
        batch = parity * 2 + n
        first = pl.multiple_of(batch * 256, 256)
        for yt in range(2):
            rows = lat[yt, parity, 4 * n : 4 * n + 4].reshape(256, 128)
            kv[yt, pl.ds(first, 256), 0:128] = rows
            both = dot(rows, gg[...])
            cross = both[:, 0:128] + both[:, 128:256] + hr2[pl.ds(first, 256), :]
            total = dot_t(ones, rows.astype(F32) * cross, lax.Precision.HIGHEST)[0:1]
            total = total + nlane[batch]
            key_scale[yt, batch] = lax.rsqrt(
                jnp.maximum(total, 0.0) * F32(1 / 3072) + F32(1e-06)
            )

    for n in range(2):
        for idx in range(4 * n, 4 * n + 4):
            block = lat.at[:, r, idx]
            pltpu.make_async_copy(block, block, rz.at[idx]).wait()
            forward(idx).start()
        take_batch(r, n)
    for n in range(2):
        for idx in range(4 * n, 4 * n + 4):
            forwarded(idx).wait_recv()
        take_batch(1 - r, n)

    tokens = []
    scales = []
    for p in range(4):
        d = place_of(p)
        patch = pl.multiple_of(((d % 2) * 2 + r) * 32, 32)
        chosen = dot(sel_q[p], kv[d // 4, :, 0:128])
        lat_q[32 * p : 32 * p + 32, :] = chosen.astype(BF16)
        both = dot(chosen.astype(BF16), gg[...])
        squares = chosen * (both[:, 0:128] + both[:, 128:256] + he2[pl.ds(patch, 32), :])
        total = jnp.sum(squares, axis=1, keepdims=True) + ncol[pl.ds(patch, 32), 0:1]
        scales.append(
            lax.rsqrt(jnp.maximum(total, 0.0) * F32(1 / 3072) + F32(1e-06))
            * F32(1 / HS**0.5)
        )
        place = (iota((32, 128), 0) + patch == iota((32, 128), 1)).astype(F32).astype(BF16)
        tokens.append(jnp.concatenate([chosen.astype(BF16), place], axis=1))
    tokens = jnp.concatenate(tokens, axis=0)
    scales = jnp.concatenate(scales, axis=0)
    pltpu.make_async_remote_copy(
        m_all.at[1 - r], m_all.at[1 - r], sp.at[1], rp.at[1], partner, MESH
    ).wait_recv()
    for role in range(2):
        q = (dot(tokens, m_all[role, 0]) + dot(tokens, m_all[role, 1])) * scales
        for h in range(2):
            q_all[2 * role + h] = q[:, 256 * h : 256 * h + 256].astype(BF16)

    width = 3072 // CHUNKS

    def copy_c(c, p):
        return pltpu.make_async_remote_copy(
            send_c.at[c, p], recv_c.at[c, p], sc.at[c, p], rc.at[c, p], ring(place_of(p), r), MESH
        )

    def land_c(c, p):
        return pltpu.make_async_remote_copy(
            send_c.at[c, p], recv_c.at[c, p], sc.at[c, p], rc.at[c, p], ring(source_of(p), r), MESH
        )

    for p in range(4):
        d = place_of(p)
        yt = d // 4
        fi = (d % 4) // 2
        keys = kv[yt]
        q = q_all[:, 32 * p : 32 * p + 32, :].reshape(128, 256)
        scale = jnp.concatenate([key_scale[yt, n] for n in range(4)], axis=1)
        s = dot_t(q, keys) * scale + bias[yt, fi]
        top = jnp.max(s, axis=1, keepdims=True)
        expo = jnp.exp(s - top)
        norm = jnp.sum(expo, axis=1, keepdims=True)
        u = dot((expo * scale).astype(BF16), keys) / norm
        u_all[:, 32 * p : 32 * p + 32, :] = u.reshape(4, 32, 256)
    pltpu.make_async_remote_copy(
        fv_all.at[1 - r], fv_all.at[1 - r], sp.at[2], rp.at[2], partner, MESH
    ).wait_recv()
    pltpu.make_async_remote_copy(
        wo.at[1 - r], wo.at[1 - r], sp.at[0], rp.at[0], partner, MESH
    ).wait_recv()
    for role in range(2):
        for h in range(2):
            hi, lo = split2(u_all[2 * role + h])
            cols = slice(HS * h, HS * h + HS)
            v_hi = fv_all[role, 0, :, cols]
            v_lo = fv_all[role, 1, :, cols]
            a = dot(hi, v_hi) + dot(lo, v_hi) + dot(hi, v_lo)
            a_all[:, 256 * role + HS * h : 256 * role + HS * h + HS] = a.astype(BF16)
    for c in range(CHUNKS):
        cols = slice(width * c, width * c + width)
        part = dot(a_all[:, 0:256], wo[0, :, cols]) + dot(a_all[:, 256:512], wo[1, :, cols])
        send_c[c] = part[0:96].reshape(3, 32, width).astype(BF16)
        acc[c] = part[96:128]
        for p in range(3):
            copy_c(c, p).start()

    own_lat = lat_q[96:128, :]
    own_patch = pl.multiple_of(((m % 2) * 2 + r) * 32, 32)
    for c in range(CHUNKS):
        cols = slice(width * c, width * c + width)
        embedded = dot(own_lat, e[:, cols]) + pos[pl.ds(own_patch, 32), cols].astype(F32)
        acc[c] = acc[c] + embedded
    outs = []
    for c in range(CHUNKS):
        cols = slice(width * c, width * c + width)
        total = acc[c]
        for p in (1, 2, 0):
            land_c(c, p).wait_recv()
            total = total + recv_c[c, p].astype(F32)
        out_ref[:, cols] = total.astype(BF16)
        outs.append(
            pltpu.make_async_copy(out_ref.at[:, cols], out_hbm.at[:, cols], out_sem.at[c])
        )
        outs[-1].start()

    for step in range(1, 8):
        copy_a(step).wait_send()
        copy_x(step).wait_send()
        copy_z(step).wait_send()

    @pl.when(jnp.logical_not(is_self))
    def _():
        copy_z(0).wait_send()

    for idx in range(8):
        forward(idx).wait_send()
    wo_copy.wait_send()
    m_copy.wait_send()
    f_copy.wait_send()
    for c in range(CHUNKS):
        for p in range(3):
            copy_c(c, p).wait_send()
    for copy in outs:
        copy.wait()


def on_device(
    gen_hidden,
    gen_out_weight,
    patch_order,
    frame_block,
    embed_weight,
    pos_table,
    norm_gain,
    qkv_weight,
    out_weight,
):
    any_space = pl.BlockSpec(memory_space=pl.ANY)
    dma = pltpu.SemaphoreType.DMA
    width = 3072 // CHUNKS
    scratch = [
        pltpu.VMEM((256, 384), BF16),
        pltpu.VMEM((384, 128), BF16),
        pltpu.VMEM((1, 128), jnp.int32),
        pltpu.SMEM((256,), jnp.int32),
        pltpu.VMEM((24, 128), BF16),
        pltpu.VMEM((32, 3072), BF16),
        pltpu.VMEM((128, 3072), BF16),
        pltpu.VMEM((128, 3072), BF16),
        pltpu.VMEM((3, 3072, 256), BF16),
        pltpu.VMEM((2, 256, 3072), BF16),
        pltpu.VMEM((288, 128), F32),
        pltpu.VMEM((8, 48, 128), F32),
        pltpu.VMEM((8, 48, 128), BF16),
        pltpu.VMEM((8, 48, 128), BF16),
        pltpu.VMEM((8, 16, 128), BF16),
        pltpu.VMEM((8, 16, 128), BF16),
        pltpu.VMEM((2, 64, 128), BF16),
        pltpu.VMEM((2, 2, 8, 64, 128), BF16),
        pltpu.VMEM((2, 1024, 256), BF16),
        pltpu.VMEM((512, 3072), BF16),
        pltpu.VMEM((2, 2, 256, 512), BF16),
        pltpu.VMEM((2, 2, 256, 256), BF16),
        pltpu.VMEM((4, 32, 1024), BF16),
        pltpu.VMEM((1024, 128), F32),
        pltpu.VMEM((128, 128), F32),
        pltpu.VMEM((128, 128), F32),
        pltpu.VMEM((4, 1, 256), F32),
        pltpu.VMEM((2, 2, 1, 1024), F32),
        pltpu.VMEM((2, 4, 1, 256), F32),
        pltpu.VMEM((128, 256), BF16),
        pltpu.VMEM((128, 128), BF16),
        pltpu.VMEM((4, 128, 256), BF16),
        pltpu.VMEM((4, 128, 256), F32),
        pltpu.VMEM((128, 512), BF16),
        pltpu.VMEM((CHUNKS, 32, width), F32),
        pltpu.VMEM((CHUNKS, 3, 32, width), BF16),
        pltpu.VMEM((CHUNKS, 3, 32, width), BF16),
        dma((9,)),
        dma((CHUNKS,)),
        dma((8,)),
        dma((8,)),
        dma((8,)),
        dma((8,)),
        dma((8,)),
        dma((8,)),
        dma((8,)),
        dma((8,)),
        dma((3,)),
        dma((3,)),
        dma((CHUNKS, 3)),
        dma((CHUNKS, 3)),
    ]
    return pl.pallas_call(
        kernel,
        out_shape=jax.ShapeDtypeStruct((32, 3072), BF16),
        in_specs=[any_space] * 9,
        out_specs=any_space,
        scratch_shapes=scratch,
        compiler_params=pltpu.CompilerParams(collective_id=0, has_side_effects=True),
    )(
        gen_hidden.reshape(256, 384),
        gen_out_weight,
        patch_order.reshape(1, 128),
        frame_block,
        embed_weight,
        pos_table,
        norm_gain.reshape(24, 128),
        jnp.transpose(qkv_weight, (1, 0, 2)),
        out_weight,
    )


def solution(mesh):
    in_specs = (
        P("seq", None, ("mp", "role")),
        P(("mp", "role"), None),
        P(),
        P(),
        P(),
        P(),
        P(),
        P(None, None, ("mp", "role")),
        P(("mp", "role"), None),
    )
    out_specs = P(("seq", "mp", "role"), None)
    return jax.shard_map(
        on_device, mesh=mesh, in_specs=in_specs, out_specs=out_specs, check_vma=False
    )
```

```python
import functools

import jax
import jax.numpy as jnp
from jax import lax
from jax.experimental import pallas as pl
from jax.experimental.pallas import tpu as pltpu
from jax.sharding import PartitionSpec as P

MESH = pl.DeviceIdType.MESH
F32 = jnp.float32
BF16 = jnp.bfloat16
HS = 128
CHUNKS = 4
NEG = -1e30


def dot(a, b, precision=None):
    return jnp.dot(a, b, preferred_element_type=F32, precision=precision)


def dot_t(a, b, precision=None):
    return lax.dot_general(
        a, b, (((1,), (1,)), ((), ())), preferred_element_type=F32, precision=precision
    )


def split2(a):
    hi = a.astype(BF16)
    return hi, (a - hi.astype(F32)).astype(BF16)


def iota(shape, dim):
    return lax.broadcasted_iota(jnp.int32, shape, dim)


def slot_of(row):
    part = lax.shift_right_logical(row, 3)
    parity = lax.shift_right_logical(part, 6)
    half = jnp.bitwise_and(lax.shift_right_logical(part, 5), 1)
    rest = jnp.bitwise_and(lax.shift_right_logical(part, 3), 3)
    return half * 64 + rest * 16 + parity * 8 + jnp.bitwise_and(part, 7)


def kernel(
    gh_hbm,
    gw_hbm,
    po_hbm,
    fb_hbm,
    e_hbm,
    pos_hbm,
    gain_hbm,
    w_hbm,
    wo_hbm,
    out_hbm,
    gh,
    gw,
    po_ref,
    fb_ref,
    gain_ref,
    out_ref,
    e,
    pos,
    w,
    wo,
    ppad,
    mine,
    send_a,
    recv_a,
    send_x,
    recv_x,
    send_z,
    lat,
    kv,
    fhl,
    m_all,
    fv_all,
    sel_q,
    hr2,
    he2,
    ncol,
    nlane,
    bias,
    key_scale,
    gg,
    lat_q,
    q_all,
    u_all,
    a_all,
    acc,
    send_c,
    recv_c,
    entered,
    allowed,
    load_sem,
    out_sem,
    sa,
    ra,
    sx,
    rx,
    sz,
    rz,
    sf,
    rf,
    sp,
    rp,
    sc,
    rc,
):
    seq = lax.axis_index("seq")
    m = lax.axis_index("mp")
    r = lax.axis_index("role")
    ys = seq // 64
    z = (seq // 8) % 8
    x = seq % 8
    j = 2 * m + r
    y = ys * 4 + m
    is_self = jnp.logical_and(j == z, True)

    def group(k):
        return (seq, k // 2, k % 2)

    def row_x(x2):
        return (ys * 64 + z * 8 + x2, m, r)

    def ring(y2, role):
        return ((y2 // 4) * 64 + z * 8 + x, y2 % 4, role)

    def row_z(z2):
        return (ys * 64 + z2 * 8 + x, m, r)

    def zy_dest(i):
        y2 = (y + i) % 8
        return ((y2 // 4) * 64 + j * 8 + x, y2 % 4, z % 2)

    side = 1 - 2 * r
    offsets = (2, -1, 1, 0)

    def place_of(p):
        return (y + side * offsets[p] + 8) % 8

    partner = (seq, m, 1 - r)

    def load(src, dst, n):
        return pltpu.make_async_copy(src, dst, load_sem.at[n])

    load_gh = load(gh_hbm, gh, 0)
    load_gw = load(gw_hbm, gw, 1)
    load_po = load(po_hbm, po_ref, 2)
    load_fb = load(fb_hbm, fb_ref, 3)
    load_gain = load(gain_hbm, gain_ref, 4)
    load_e = load(e_hbm, e, 5)
    load_pos = load(pos_hbm, pos, 6)
    load_w = load(w_hbm, w, 7)
    load_wo = load(wo_hbm, wo.at[r], 8)
    load_gh.start()
    load_gw.start()

    barrier = pltpu.get_barrier_semaphore()

    def greet(device):
        pl.semaphore_signal(barrier, inc=1, device_id=device, device_id_type=MESH)

    for step in range(1, 8):
        greet(row_z((z + step) % 8))
        greet(row_x((x + step) % 8))
    for step in range(1, 8):
        greet(ring((y + step) % 8, r))
    for step in range(8):
        greet(ring((y + step) % 8, 1 - r))

    for copy in (load_po, load_fb, load_gain):
        copy.start()
    ppad[0:8, :] = jnp.zeros((8, 128), F32)
    ppad[264:288, :] = jnp.zeros((24, 128), F32)

    load_gh.wait()
    load_gw.wait()
    ppad[8:264, :] = dot(gh[...], gw[...])
    for k in range(8):
        parts = [ppad[128 * yt + 16 * k + 5 : 128 * yt + 16 * k + 29, :] for yt in range(2)]
        part = jnp.concatenate(parts, axis=0)
        mine[k] = part
        send_a[k] = part.astype(BF16)

    pl.semaphore_wait(barrier, 29)

    def copy_a(step):
        k = (j + step) % 8
        return pltpu.make_async_remote_copy(
            send_a.at[k], recv_a.at[j], sa.at[step], ra.at[j], group(k), MESH
        )

    def land_a(step):
        k = (j + step) % 8
        return pltpu.make_async_remote_copy(
            send_a.at[k], recv_a.at[k], sa.at[step], ra.at[k], group(k), MESH
        )

    for step in range(1, 8):
        copy_a(step).start()
    for z2 in range(8):

        @pl.when(jnp.logical_and(z2 != z, r == z2 % 2))
        def _():
            pl.semaphore_signal(entered.at[z], inc=1, device_id=row_z(z2), device_id_type=MESH)

    for copy in (load_e, load_pos, load_w, load_wo):
        copy.start()
    wo_copy = pltpu.make_async_remote_copy(
        wo_hbm, wo.at[r], sp.at[0], rp.at[0], partner, MESH
    )
    wo_copy.start()

    load_po.wait()
    load_fb.wait()
    po_f = jnp.broadcast_to(po_ref[...], (16, 128)).astype(F32).astype(BF16)
    spread = (iota((128, 1024), 0) == slot_of(iota((128, 1024), 1))).astype(F32).astype(BF16)
    po_lane = dot(po_f, spread)[0:1]
    perm_t = (jnp.broadcast_to(po_ref[...], (128, 128)) == iota((128, 128), 0)).astype(F32).astype(
        BF16
    )
    rows8 = (slot_of(iota((1024, 128), 0)) == iota((1024, 128), 1)).astype(F32).astype(BF16)
    onehot = dot_t(rows8, perm_t).astype(BF16)
    kv[0, :, 128:256] = onehot
    kv[1, :, 128:256] = onehot
    w_lane = jnp.bitwise_and(iota((1, 1024), 1), 7)
    for yt in range(2):
        base = yt * 128 + z * 16 + x * 2 - 3
        blocks = []
        key_block = jnp.full((1, 1024), -1, jnp.int32)
        for n in range(8):
            frame = base + n
            value = fb_ref[jnp.clip(frame, 0, 255)]
            value = jnp.where(jnp.logical_and(frame >= 0, frame <= 255), value, -1)
            blocks.append(value)
            key_block = jnp.where(w_lane == n, value, key_block)
        for fi in range(2):
            bias[yt, fi] = jnp.where(key_block == blocks[3 + fi], F32(0), F32(NEG))
    for p in range(4):
        d = place_of(p)
        fi = (d % 4) // 2
        patch = ((d % 2) * 2 + r) * 32
        rows = (iota((32, 1024), 0) + patch).astype(F32)
        hit = jnp.logical_and(
            jnp.broadcast_to(po_lane, (32, 1024)) == rows,
            jnp.broadcast_to(w_lane, (32, 1024)) == 3 + fi,
        )
        sel_q[p] = hit.astype(F32).astype(BF16)

    load_e.wait()
    load_pos.wait()
    load_gain.wait()
    gain = gain_ref[...].astype(F32)
    for n, table in enumerate((e, pos)):
        for part in range(24):
            cols = slice(128 * part, 128 * part + 128)
            hi, lo = split2(table[:, cols].astype(F32) * gain[part : part + 1, :])
            fhl[n * 128 : n * 128 + 128, cols] = hi
            fhl[256 + n * 128 : 384 + n * 128, cols] = lo
    ghi, glo = split2(dot_t(e[...], e[...]))
    gg[:, 0:128] = ghi
    gg[:, 128:256] = glo
    he = 2.0 * dot_t(pos[...], e[...])
    he2[...] = he
    he_hi, he_lo = split2(he)
    hr2[...] = dot(onehot, he_hi) + dot(onehot, he_lo)
    norms = dot_t(pos[...], pos[...])
    diagonal = jnp.where(iota((128, 128), 0) == iota((128, 128), 1), norms, F32(0))
    ncol[...] = jnp.broadcast_to(jnp.sum(diagonal, axis=1, keepdims=True), (128, 128))
    nrow = jnp.broadcast_to(jnp.sum(diagonal, axis=0, keepdims=True), (8, 128))
    norm_lane = dot_t(nrow, onehot.astype(F32), lax.Precision.HIGHEST)[0:1]
    for n in range(4):
        nlane[n] = norm_lane[:, 256 * n : 256 * n + 256]
    load_w.wait()
    load_wo.wait()

    def weight_product(c):
        both = dot(fhl[...], w[c])
        return both[0:256] + both[256:512]

    for step in range(1, 8):
        land_a(step).wait_recv()
    @pl.when(r == z % 2)
    def _():
        for z2 in range(8):

            @pl.when(z2 != z)
            def _():
                pl.semaphore_wait(entered.at[z2], 1)

            for half_y in range(2):

                @pl.when(jnp.logical_not(jnp.logical_and(ys == half_y, j == z2)))
                def _():
                    pl.semaphore_signal(
                        allowed,
                        inc=1,
                        device_id=(half_y * 64 + z * 8 + x, z2 // 2, z2 % 2),
                        device_id_type=MESH,
                    )

    total = mine[j]
    for step in range(1, 8):
        total = total + recv_a[(j + step) % 8].astype(F32)
    mine[j] = total
    for n in range(8):
        halves = [mine[j, 24 * yt + 2 * n : 24 * yt + 2 * n + 8, :] for yt in range(2)]
        send_x[n] = jnp.concatenate(halves, axis=0).astype(BF16)

    def copy_x(step):
        x2 = (x + step) % 8
        return pltpu.make_async_remote_copy(
            send_x.at[x2], recv_x.at[x], sx.at[step], rx.at[x], row_x(x2), MESH
        )

    def land_x(step):
        x2 = (x + step) % 8
        return pltpu.make_async_remote_copy(
            send_x.at[x2], recv_x.at[x2], sx.at[step], rx.at[x2], row_x(x2), MESH
        )

    for step in range(1, 8):
        copy_x(step).start()
    recv_x[x] = send_x[x]

    fq = weight_product(0)
    fk = weight_product(1)

    for step in range(1, 8):
        land_x(step).wait_recv()
    for a in range(4):
        first = recv_x[2 * a].astype(F32)
        second = recv_x[2 * a + 1].astype(F32)
        for yt in range(2):
            pair = jnp.concatenate(
                [first[8 * yt : 8 * yt + 8], second[8 * yt : 8 * yt + 8]], axis=0
            )
            send_z[yt, 16 * a : 16 * a + 16, :] = pair.astype(BF16)

    half = z % 2
    own_idx = ys * 4 + z // 2

    def copy_z(i):
        return pltpu.make_async_remote_copy(
            send_z, lat.at[:, half, own_idx], sz.at[i], rz.at[own_idx], zy_dest(i), MESH
        )

    local_z = pltpu.make_async_copy(send_z, lat.at[:, half, own_idx], rz.at[own_idx])
    pl.semaphore_wait(allowed, 8 - (r == z % 2).astype(jnp.int32))
    for i in range(1, 8):
        copy_z(i).start()

    @pl.when(jnp.logical_not(is_self))
    def _():
        copy_z(0).start()

    @pl.when(is_self)
    def _():
        local_z.start()

    for h in range(2):
        cols = slice(HS * h, HS * h + HS)
        bil = dot_t(fq[:, cols], fk[:, cols], lax.Precision.HIGHEST)
        hi, lo = split2(bil)
        m_all[r, 0, :, 256 * h : 256 * h + 256] = hi
        m_all[r, 1, :, 256 * h : 256 * h + 256] = lo
    hi, lo = split2(weight_product(2))
    fv_all[r, 0] = hi
    fv_all[r, 1] = lo
    m_copy = pltpu.make_async_remote_copy(
        m_all.at[r], m_all.at[r], sp.at[1], rp.at[1], partner, MESH
    )
    f_copy = pltpu.make_async_remote_copy(
        fv_all.at[r], fv_all.at[r], sp.at[2], rp.at[2], partner, MESH
    )
    m_copy.start()
    f_copy.start()

    def forward(idx):
        block = lat.at[:, r, idx]
        return pltpu.make_async_remote_copy(
            block, block, sf.at[idx], rf.at[idx], partner, MESH
        )

    def forwarded(idx):
        block = lat.at[:, 1 - r, idx]
        return pltpu.make_async_remote_copy(
            block, block, sf.at[idx], rf.at[idx], partner, MESH
        )

    ones = jnp.ones((8, 128), F32)

    def take_batch(parity, n):
        batch = parity * 2 + n
        first = pl.multiple_of(batch * 256, 256)
        for yt in range(2):
            rows = lat[yt, parity, 4 * n : 4 * n + 4].reshape(256, 128)
            kv[yt, pl.ds(first, 256), 0:128] = rows
            both = dot(rows, gg[...])
            cross = both[:, 0:128] + both[:, 128:256] + hr2[pl.ds(first, 256), :]
            total = dot_t(ones, rows.astype(F32) * cross, lax.Precision.HIGHEST)[0:1]
            total = total + nlane[batch]
            key_scale[yt, batch] = lax.rsqrt(
                jnp.maximum(total, 0.0) * F32(1 / 3072) + F32(1e-06)
            )

    for n in range(2):
        for idx in range(4 * n, 4 * n + 4):
            block = lat.at[:, r, idx]
            pltpu.make_async_copy(block, block, rz.at[idx]).wait()
            forward(idx).start()
        take_batch(r, n)
    for n in range(2):
        for idx in range(4 * n, 4 * n + 4):
            forwarded(idx).wait_recv()
        take_batch(1 - r, n)

    tokens = []
    scales = []
    for p in range(4):
        d = place_of(p)
        patch = pl.multiple_of(((d % 2) * 2 + r) * 32, 32)
        chosen = dot(sel_q[p], kv[d // 4, :, 0:128])
        lat_q[32 * p : 32 * p + 32, :] = chosen.astype(BF16)
        both = dot(chosen.astype(BF16), gg[...])
        squares = chosen * (both[:, 0:128] + both[:, 128:256] + he2[pl.ds(patch, 32), :])
        total = jnp.sum(squares, axis=1, keepdims=True) + ncol[pl.ds(patch, 32), 0:1]
        scales.append(
            lax.rsqrt(jnp.maximum(total, 0.0) * F32(1 / 3072) + F32(1e-06))
            * F32(1 / HS**0.5)
        )
        place = (iota((32, 128), 0) + patch == iota((32, 128), 1)).astype(F32).astype(BF16)
        tokens.append(jnp.concatenate([chosen.astype(BF16), place], axis=1))
    tokens = jnp.concatenate(tokens, axis=0)
    scales = jnp.concatenate(scales, axis=0)
    pltpu.make_async_remote_copy(
        m_all.at[1 - r], m_all.at[1 - r], sp.at[1], rp.at[1], partner, MESH
    ).wait_recv()
    for role in range(2):
        q = (dot(tokens, m_all[role, 0]) + dot(tokens, m_all[role, 1])) * scales
        for h in range(2):
            q_all[2 * role + h] = q[:, 256 * h : 256 * h + 256].astype(BF16)

    width = 3072 // CHUNKS

    def copy_c(c, p):
        step = -side if p == 1 else side
        return pltpu.make_async_remote_copy(
            send_c.at[c, p],
            recv_c.at[c, p],
            sc.at[c, p],
            rc.at[c, p],
            ring((y + step + 8) % 8, r),
            MESH,
        )

    def land_c(c, p):
        step = side if p == 1 else -side
        return pltpu.make_async_remote_copy(
            send_c.at[c, p],
            recv_c.at[c, p],
            sc.at[c, p],
            rc.at[c, p],
            ring((y + step + 8) % 8, r),
            MESH,
        )

    for p in range(4):
        d = place_of(p)
        yt = d // 4
        fi = (d % 4) // 2
        keys = kv[yt]
        q = q_all[:, 32 * p : 32 * p + 32, :].reshape(128, 256)
        scale = jnp.concatenate([key_scale[yt, n] for n in range(4)], axis=1)
        s = dot_t(q, keys) * scale + bias[yt, fi]
        top = jnp.max(s, axis=1, keepdims=True)
        expo = jnp.exp(s - top)
        norm = jnp.sum(expo, axis=1, keepdims=True)
        u = dot((expo * scale).astype(BF16), keys) / norm
        u_all[:, 32 * p : 32 * p + 32, :] = u.reshape(4, 32, 256)
    pltpu.make_async_remote_copy(
        fv_all.at[1 - r], fv_all.at[1 - r], sp.at[2], rp.at[2], partner, MESH
    ).wait_recv()
    pltpu.make_async_remote_copy(
        wo.at[1 - r], wo.at[1 - r], sp.at[0], rp.at[0], partner, MESH
    ).wait_recv()
    for role in range(2):
        for h in range(2):
            hi, lo = split2(u_all[2 * role + h])
            cols = slice(HS * h, HS * h + HS)
            v_hi = fv_all[role, 0, :, cols]
            v_lo = fv_all[role, 1, :, cols]
            a = dot(hi, v_hi) + dot(lo, v_hi) + dot(hi, v_lo)
            a_all[:, 256 * role + HS * h : 256 * role + HS * h + HS] = a.astype(BF16)
    for c in range(CHUNKS):
        cols = slice(width * c, width * c + width)
        part = dot(a_all[:, 0:256], wo[0, :, cols]) + dot(a_all[:, 256:512], wo[1, :, cols])
        send_c[c, 0:2] = part[0:64].reshape(2, 32, width).astype(BF16)
        acc[c] = part[64:128].reshape(2, 32, width)
        copy_c(c, 0).start()
        copy_c(c, 1).start()

    own_lat = lat_q[96:128, :]
    own_patch = pl.multiple_of(((m % 2) * 2 + r) * 32, 32)
    for c in range(CHUNKS):
        cols = slice(width * c, width * c + width)
        embedded = dot(own_lat, e[:, cols]) + pos[pl.ds(own_patch, 32), cols].astype(F32)
        acc[c, 1] = acc[c, 1] + embedded
    for c in range(CHUNKS):
        land_c(c, 0).wait_recv()
        send_c[c, 2] = (acc[c, 0] + recv_c[c, 0].astype(F32)).astype(BF16)
        copy_c(c, 2).start()
    outs = []
    for c in range(CHUNKS):
        cols = slice(width * c, width * c + width)
        total = acc[c, 1]
        for p in (1, 2):
            land_c(c, p).wait_recv()
            total = total + recv_c[c, p].astype(F32)
        out_ref[:, cols] = total.astype(BF16)
        outs.append(
            pltpu.make_async_copy(out_ref.at[:, cols], out_hbm.at[:, cols], out_sem.at[c])
        )
        outs[-1].start()

    for step in range(1, 8):
        copy_a(step).wait_send()
        copy_x(step).wait_send()
        copy_z(step).wait_send()

    @pl.when(jnp.logical_not(is_self))
    def _():
        copy_z(0).wait_send()

    for idx in range(8):
        forward(idx).wait_send()
    wo_copy.wait_send()
    m_copy.wait_send()
    f_copy.wait_send()
    for c in range(CHUNKS):
        for p in range(3):
            copy_c(c, p).wait_send()
    for copy in outs:
        copy.wait()


def on_device(
    gen_hidden,
    gen_out_weight,
    patch_order,
    frame_block,
    embed_weight,
    pos_table,
    norm_gain,
    qkv_weight,
    out_weight,
):
    any_space = pl.BlockSpec(memory_space=pl.ANY)
    dma = pltpu.SemaphoreType.DMA
    width = 3072 // CHUNKS
    scratch = [
        pltpu.VMEM((256, 384), BF16),
        pltpu.VMEM((384, 128), BF16),
        pltpu.VMEM((1, 128), jnp.int32),
        pltpu.SMEM((256,), jnp.int32),
        pltpu.VMEM((24, 128), BF16),
        pltpu.VMEM((32, 3072), BF16),
        pltpu.VMEM((128, 3072), BF16),
        pltpu.VMEM((128, 3072), BF16),
        pltpu.VMEM((3, 3072, 256), BF16),
        pltpu.VMEM((2, 256, 3072), BF16),
        pltpu.VMEM((288, 128), F32),
        pltpu.VMEM((8, 48, 128), F32),
        pltpu.VMEM((8, 48, 128), BF16),
        pltpu.VMEM((8, 48, 128), BF16),
        pltpu.VMEM((8, 16, 128), BF16),
        pltpu.VMEM((8, 16, 128), BF16),
        pltpu.VMEM((2, 64, 128), BF16),
        pltpu.VMEM((2, 2, 8, 64, 128), BF16),
        pltpu.VMEM((2, 1024, 256), BF16),
        pltpu.VMEM((512, 3072), BF16),
        pltpu.VMEM((2, 2, 256, 512), BF16),
        pltpu.VMEM((2, 2, 256, 256), BF16),
        pltpu.VMEM((4, 32, 1024), BF16),
        pltpu.VMEM((1024, 128), F32),
        pltpu.VMEM((128, 128), F32),
        pltpu.VMEM((128, 128), F32),
        pltpu.VMEM((4, 1, 256), F32),
        pltpu.VMEM((2, 2, 1, 1024), F32),
        pltpu.VMEM((2, 4, 1, 256), F32),
        pltpu.VMEM((128, 256), BF16),
        pltpu.VMEM((128, 128), BF16),
        pltpu.VMEM((4, 128, 256), BF16),
        pltpu.VMEM((4, 128, 256), F32),
        pltpu.VMEM((128, 512), BF16),
        pltpu.VMEM((CHUNKS, 2, 32, width), F32),
        pltpu.VMEM((CHUNKS, 3, 32, width), BF16),
        pltpu.VMEM((CHUNKS, 3, 32, width), BF16),
        pltpu.SemaphoreType.REGULAR((8,)),
        pltpu.SemaphoreType.REGULAR,
        dma((9,)),
        dma((CHUNKS,)),
        dma((8,)),
        dma((8,)),
        dma((8,)),
        dma((8,)),
        dma((8,)),
        dma((8,)),
        dma((8,)),
        dma((8,)),
        dma((3,)),
        dma((3,)),
        dma((CHUNKS, 3)),
        dma((CHUNKS, 3)),
    ]
    return pl.pallas_call(
        kernel,
        out_shape=jax.ShapeDtypeStruct((32, 3072), BF16),
        in_specs=[any_space] * 9,
        out_specs=any_space,
        scratch_shapes=scratch,
        compiler_params=pltpu.CompilerParams(collective_id=0, has_side_effects=True),
    )(
        gen_hidden.reshape(256, 384),
        gen_out_weight,
        patch_order.reshape(1, 128),
        frame_block,
        embed_weight,
        pos_table,
        norm_gain.reshape(24, 128),
        jnp.transpose(qkv_weight, (1, 0, 2)),
        out_weight,
    )


def solution(mesh):
    in_specs = (
        P("seq", None, ("mp", "role")),
        P(("mp", "role"), None),
        P(),
        P(),
        P(),
        P(),
        P(),
        P(None, None, ("mp", "role")),
        P(("mp", "role"), None),
    )
    out_specs = P(("seq", "mp", "role"), None)
    return jax.shard_map(
        on_device, mesh=mesh, in_specs=in_specs, out_specs=out_specs, check_vma=False
    )
```

```python
import functools

import jax
import jax.numpy as jnp
from jax import lax
from jax.experimental import pallas as pl
from jax.experimental.pallas import tpu as pltpu
from jax.sharding import PartitionSpec as P

MESH = pl.DeviceIdType.MESH
F32 = jnp.float32
BF16 = jnp.bfloat16
HS = 128
CHUNKS = 4
NEG = -1e30


def dot(a, b, precision=None):
    return jnp.dot(a, b, preferred_element_type=F32, precision=precision)


def dot_t(a, b, precision=None):
    return lax.dot_general(
        a, b, (((1,), (1,)), ((), ())), preferred_element_type=F32, precision=precision
    )


def split2(a):
    hi = a.astype(BF16)
    return hi, (a - hi.astype(F32)).astype(BF16)


def iota(shape, dim):
    return lax.broadcasted_iota(jnp.int32, shape, dim)


def slot_of(row):
    part = lax.shift_right_logical(row, 3)
    parity = lax.shift_right_logical(part, 6)
    half = jnp.bitwise_and(lax.shift_right_logical(part, 5), 1)
    rest = jnp.bitwise_and(lax.shift_right_logical(part, 3), 3)
    return half * 64 + rest * 16 + parity * 8 + jnp.bitwise_and(part, 7)


def kernel(
    gh_hbm,
    gw_hbm,
    po_hbm,
    fb_hbm,
    e_hbm,
    pos_hbm,
    gain_hbm,
    w_hbm,
    wo_hbm,
    out_hbm,
    gh,
    gw,
    po_ref,
    fb_ref,
    gain_ref,
    out_ref,
    e,
    pos,
    w,
    wo,
    ppad,
    mine,
    send_a,
    recv_a,
    send_x,
    recv_x,
    send_z,
    lat,
    kv,
    fhl,
    m_all,
    fv_all,
    sel_q,
    hr2,
    he2,
    ncol,
    nlane,
    bias,
    key_scale,
    gg,
    lat_q,
    q_all,
    u_all,
    a_all,
    acc,
    send_c,
    recv_c,
    entered,
    allowed,
    load_sem,
    out_sem,
    sa,
    ra,
    sx,
    rx,
    sz,
    rz,
    sf,
    rf,
    sp,
    rp,
    sc,
    rc,
):
    seq = lax.axis_index("seq")
    m = lax.axis_index("mp")
    r = lax.axis_index("role")
    ys = seq // 64
    z = (seq // 8) % 8
    x = seq % 8
    j = 2 * m + r
    y = ys * 4 + m
    is_self = jnp.logical_and(j == z, True)

    def group(k):
        return (seq, k // 2, k % 2)

    def row_x(x2):
        return (ys * 64 + z * 8 + x2, m, r)

    def ring(y2, role):
        return ((y2 // 4) * 64 + z * 8 + x, y2 % 4, role)

    def row_z(z2):
        return (ys * 64 + z2 * 8 + x, m, r)

    def zy_dest(i):
        y2 = (y + i) % 8
        return ((y2 // 4) * 64 + j * 8 + x, y2 % 4, z % 2)

    side = 1 - 2 * r
    offsets = (2, -1, 1, 0)

    def place_of(p):
        return (y + side * offsets[p] + 8) % 8

    partner = (seq, m, 1 - r)

    def load(src, dst, n):
        return pltpu.make_async_copy(src, dst, load_sem.at[n])

    load_gh = load(gh_hbm, gh, 0)
    load_gw = load(gw_hbm, gw, 1)
    load_po = load(po_hbm, po_ref, 2)
    load_fb = load(fb_hbm, fb_ref, 3)
    load_gain = load(gain_hbm, gain_ref, 4)
    load_e = load(e_hbm, e, 5)
    load_pos = load(pos_hbm, pos, 6)
    load_w = load(w_hbm, w, 7)
    load_wo = load(wo_hbm, wo.at[r], 8)
    load_gh.start()
    load_gw.start()

    barrier = pltpu.get_barrier_semaphore()

    def greet(device):
        pl.semaphore_signal(barrier, inc=1, device_id=device, device_id_type=MESH)

    for step in range(1, 8):
        greet(row_z((z + step) % 8))
        greet(row_x((x + step) % 8))
    for step in range(1, 8):
        greet(ring((y + step) % 8, r))
    for step in range(8):
        greet(ring((y + step) % 8, 1 - r))

    for copy in (load_po, load_fb, load_gain):
        copy.start()
    ppad[0:8, :] = jnp.zeros((8, 128), F32)
    ppad[264:288, :] = jnp.zeros((24, 128), F32)

    load_gh.wait()
    load_gw.wait()
    ppad[8:264, :] = dot(gh[...], gw[...])
    for k in range(8):
        parts = [ppad[128 * yt + 16 * k + 5 : 128 * yt + 16 * k + 29, :] for yt in range(2)]
        part = jnp.concatenate(parts, axis=0)
        mine[k] = part
        send_a[k] = part.astype(BF16)

    pl.semaphore_wait(barrier, 29)

    def copy_a(step):
        k = (j + step) % 8
        return pltpu.make_async_remote_copy(
            send_a.at[k], recv_a.at[j], sa.at[step], ra.at[j], group(k), MESH
        )

    def land_a(step):
        k = (j + step) % 8
        return pltpu.make_async_remote_copy(
            send_a.at[k], recv_a.at[k], sa.at[step], ra.at[k], group(k), MESH
        )

    for step in range(1, 8):
        copy_a(step).start()
    for z2 in range(8):

        @pl.when(jnp.logical_and(z2 != z, r == z2 % 2))
        def _():
            pl.semaphore_signal(entered.at[z], inc=1, device_id=row_z(z2), device_id_type=MESH)

    for copy in (load_e, load_pos, load_w, load_wo):
        copy.start()
    wo_copy = pltpu.make_async_remote_copy(
        wo_hbm, wo.at[r], sp.at[0], rp.at[0], partner, MESH
    )
    wo_copy.start()

    load_po.wait()
    load_fb.wait()
    po_f = jnp.broadcast_to(po_ref[...], (16, 128)).astype(F32).astype(BF16)
    spread = (iota((128, 1024), 0) == slot_of(iota((128, 1024), 1))).astype(F32).astype(BF16)
    po_lane = dot(po_f, spread)[0:1]
    perm_t = (jnp.broadcast_to(po_ref[...], (128, 128)) == iota((128, 128), 0)).astype(F32).astype(
        BF16
    )
    rows8 = (slot_of(iota((1024, 128), 0)) == iota((1024, 128), 1)).astype(F32).astype(BF16)
    onehot = dot_t(rows8, perm_t).astype(BF16)
    kv[0, :, 128:256] = onehot
    kv[1, :, 128:256] = onehot
    w_lane = jnp.bitwise_and(iota((1, 1024), 1), 7)
    for yt in range(2):
        base = yt * 128 + z * 16 + x * 2 - 3
        blocks = []
        key_block = jnp.full((1, 1024), -1, jnp.int32)
        for n in range(8):
            frame = base + n
            value = fb_ref[jnp.clip(frame, 0, 255)]
            value = jnp.where(jnp.logical_and(frame >= 0, frame <= 255), value, -1)
            blocks.append(value)
            key_block = jnp.where(w_lane == n, value, key_block)
        for fi in range(2):
            bias[yt, fi] = jnp.where(key_block == blocks[3 + fi], F32(0), F32(NEG))
    for p in range(4):
        d = place_of(p)
        fi = (d % 4) // 2
        patch = ((d % 2) * 2 + r) * 32
        rows = (iota((32, 1024), 0) + patch).astype(F32)
        hit = jnp.logical_and(
            jnp.broadcast_to(po_lane, (32, 1024)) == rows,
            jnp.broadcast_to(w_lane, (32, 1024)) == 3 + fi,
        )
        sel_q[p] = hit.astype(F32).astype(BF16)

    def weight_product(c):
        both = dot(fhl[...], w[c])
        return both[0:256] + both[256:512]

    for step in range(1, 8):
        land_a(step).wait_recv()
    @pl.when(r == z % 2)
    def _():
        for z2 in range(8):

            @pl.when(z2 != z)
            def _():
                pl.semaphore_wait(entered.at[z2], 1)

            for half_y in range(2):

                @pl.when(jnp.logical_not(jnp.logical_and(ys == half_y, j == z2)))
                def _():
                    pl.semaphore_signal(
                        allowed,
                        inc=1,
                        device_id=(half_y * 64 + z * 8 + x, z2 // 2, z2 % 2),
                        device_id_type=MESH,
                    )

    total = mine[j]
    for step in range(1, 8):
        total = total + recv_a[(j + step) % 8].astype(F32)
    mine[j] = total
    for n in range(8):
        halves = [mine[j, 24 * yt + 2 * n : 24 * yt + 2 * n + 8, :] for yt in range(2)]
        send_x[n] = jnp.concatenate(halves, axis=0).astype(BF16)

    def copy_x(step):
        x2 = (x + step) % 8
        return pltpu.make_async_remote_copy(
            send_x.at[x2], recv_x.at[x], sx.at[step], rx.at[x], row_x(x2), MESH
        )

    def land_x(step):
        x2 = (x + step) % 8
        return pltpu.make_async_remote_copy(
            send_x.at[x2], recv_x.at[x2], sx.at[step], rx.at[x2], row_x(x2), MESH
        )

    for step in range(1, 8):
        copy_x(step).start()
    recv_x[x] = send_x[x]

    load_e.wait()
    load_pos.wait()
    load_gain.wait()
    gain = gain_ref[...].astype(F32)
    for n, table in enumerate((e, pos)):
        for part in range(24):
            cols = slice(128 * part, 128 * part + 128)
            hi, lo = split2(table[:, cols].astype(F32) * gain[part : part + 1, :])
            fhl[n * 128 : n * 128 + 128, cols] = hi
            fhl[256 + n * 128 : 384 + n * 128, cols] = lo
    ghi, glo = split2(dot_t(e[...], e[...]))
    gg[:, 0:128] = ghi
    gg[:, 128:256] = glo
    he = 2.0 * dot_t(pos[...], e[...])
    he2[...] = he
    he_hi, he_lo = split2(he)
    hr2[...] = dot(onehot, he_hi) + dot(onehot, he_lo)
    norms = dot_t(pos[...], pos[...])
    diagonal = jnp.where(iota((128, 128), 0) == iota((128, 128), 1), norms, F32(0))
    ncol[...] = jnp.broadcast_to(jnp.sum(diagonal, axis=1, keepdims=True), (128, 128))
    nrow = jnp.broadcast_to(jnp.sum(diagonal, axis=0, keepdims=True), (8, 128))
    norm_lane = dot_t(nrow, onehot.astype(F32), lax.Precision.HIGHEST)[0:1]
    for n in range(4):
        nlane[n] = norm_lane[:, 256 * n : 256 * n + 256]
    load_w.wait()
    load_wo.wait()

    for step in range(1, 8):
        land_x(step).wait_recv()
    for a in range(4):
        first = recv_x[2 * a].astype(F32)
        second = recv_x[2 * a + 1].astype(F32)
        for yt in range(2):
            pair = jnp.concatenate(
                [first[8 * yt : 8 * yt + 8], second[8 * yt : 8 * yt + 8]], axis=0
            )
            send_z[yt, 16 * a : 16 * a + 16, :] = pair.astype(BF16)

    half = z % 2
    own_idx = ys * 4 + z // 2

    def copy_z(i):
        return pltpu.make_async_remote_copy(
            send_z, lat.at[:, half, own_idx], sz.at[i], rz.at[own_idx], zy_dest(i), MESH
        )

    local_z = pltpu.make_async_copy(send_z, lat.at[:, half, own_idx], rz.at[own_idx])
    pl.semaphore_wait(allowed, 8 - (r == z % 2).astype(jnp.int32))
    for i in range(1, 8):
        copy_z(i).start()

    @pl.when(jnp.logical_not(is_self))
    def _():
        copy_z(0).start()

    @pl.when(is_self)
    def _():
        local_z.start()

    fq = weight_product(0)
    fk = weight_product(1)
    for h in range(2):
        cols = slice(HS * h, HS * h + HS)
        bil = dot_t(fq[:, cols], fk[:, cols], lax.Precision.HIGHEST)
        hi, lo = split2(bil)
        m_all[r, 0, :, 256 * h : 256 * h + 256] = hi
        m_all[r, 1, :, 256 * h : 256 * h + 256] = lo
    hi, lo = split2(weight_product(2))
    fv_all[r, 0] = hi
    fv_all[r, 1] = lo
    m_copy = pltpu.make_async_remote_copy(
        m_all.at[r], m_all.at[r], sp.at[1], rp.at[1], partner, MESH
    )
    f_copy = pltpu.make_async_remote_copy(
        fv_all.at[r], fv_all.at[r], sp.at[2], rp.at[2], partner, MESH
    )
    m_copy.start()
    f_copy.start()

    def forward(idx):
        block = lat.at[:, r, idx]
        return pltpu.make_async_remote_copy(
            block, block, sf.at[idx], rf.at[idx], partner, MESH
        )

    def forwarded(idx):
        block = lat.at[:, 1 - r, idx]
        return pltpu.make_async_remote_copy(
            block, block, sf.at[idx], rf.at[idx], partner, MESH
        )

    ones = jnp.ones((16, 128), F32).astype(BF16)

    def take_batch(parity, n):
        batch = parity * 2 + n
        first = pl.multiple_of(batch * 256, 256)
        for yt in range(2):
            rows = lat[yt, parity, 4 * n : 4 * n + 4].reshape(256, 128)
            kv[yt, pl.ds(first, 256), 0:128] = rows
            both = dot(rows, gg[...])
            cross = both[:, 0:128] + both[:, 128:256] + hr2[pl.ds(first, 256), :]
            hi, lo = split2(rows.astype(F32) * cross)
            total = dot_t(ones, hi)[0:1] + dot_t(ones, lo)[0:1] + nlane[batch]
            key_scale[yt, batch] = lax.rsqrt(
                jnp.maximum(total, 0.0) * F32(1 / 3072) + F32(1e-06)
            )

    for n in range(2):
        for idx in range(4 * n, 4 * n + 4):
            block = lat.at[:, r, idx]
            pltpu.make_async_copy(block, block, rz.at[idx]).wait()
            forward(idx).start()
        take_batch(r, n)
        for idx in range(4 * n, 4 * n + 4):
            forwarded(idx).wait_recv()
        take_batch(1 - r, n)

    tokens = []
    scales = []
    for p in range(4):
        d = place_of(p)
        patch = pl.multiple_of(((d % 2) * 2 + r) * 32, 32)
        chosen = dot(sel_q[p], kv[d // 4, :, 0:128])
        lat_q[32 * p : 32 * p + 32, :] = chosen.astype(BF16)
        both = dot(chosen.astype(BF16), gg[...])
        squares = chosen * (both[:, 0:128] + both[:, 128:256] + he2[pl.ds(patch, 32), :])
        total = jnp.sum(squares, axis=1, keepdims=True) + ncol[pl.ds(patch, 32), 0:1]
        scales.append(
            lax.rsqrt(jnp.maximum(total, 0.0) * F32(1 / 3072) + F32(1e-06))
            * F32(1 / HS**0.5)
        )
        place = (iota((32, 128), 0) + patch == iota((32, 128), 1)).astype(F32).astype(BF16)
        tokens.append(jnp.concatenate([chosen.astype(BF16), place], axis=1))
    tokens = jnp.concatenate(tokens, axis=0)
    scales = jnp.concatenate(scales, axis=0)
    pltpu.make_async_remote_copy(
        m_all.at[1 - r], m_all.at[1 - r], sp.at[1], rp.at[1], partner, MESH
    ).wait_recv()
    for role in range(2):
        q = (dot(tokens, m_all[role, 0]) + dot(tokens, m_all[role, 1])) * scales
        for h in range(2):
            q_all[2 * role + h] = q[:, 256 * h : 256 * h + 256].astype(BF16)

    width = 3072 // CHUNKS

    def copy_c(c, p):
        step = -side if p == 1 else side
        return pltpu.make_async_remote_copy(
            send_c.at[c, p],
            recv_c.at[c, p],
            sc.at[c, p],
            rc.at[c, p],
            ring((y + step + 8) % 8, r),
            MESH,
        )

    def land_c(c, p):
        step = side if p == 1 else -side
        return pltpu.make_async_remote_copy(
            send_c.at[c, p],
            recv_c.at[c, p],
            sc.at[c, p],
            rc.at[c, p],
            ring((y + step + 8) % 8, r),
            MESH,
        )

    def attend(p):
        d = place_of(p)
        yt = d // 4
        fi = (d % 4) // 2
        keys = kv[yt]
        q = q_all[:, 32 * p : 32 * p + 32, :].reshape(128, 256)
        scale = jnp.concatenate([key_scale[yt, n] for n in range(4)], axis=1)
        s = dot_t(q, keys) * scale + bias[yt, fi]
        top = jnp.max(s, axis=1, keepdims=True)
        expo = jnp.exp(s - top)
        norm = jnp.sum(expo, axis=1, keepdims=True)
        u = dot((expo * scale).astype(BF16), keys) / norm
        u_all[:, 32 * p : 32 * p + 32, :] = u.reshape(4, 32, 256)

    def heads_out(rows):
        for role in range(2):
            for h in range(2):
                hi, lo = split2(u_all[2 * role + h, rows, :])
                cols = slice(HS * h, HS * h + HS)
                v_hi = fv_all[role, 0, :, cols]
                v_lo = fv_all[role, 1, :, cols]
                a = dot(hi, v_hi) + dot(lo, v_hi) + dot(hi, v_lo)
                a_all[rows, 256 * role + HS * h : 256 * role + HS * h + HS] = a.astype(BF16)

    def projected(rows, c):
        cols = slice(width * c, width * c + width)
        return dot(a_all[rows, 0:256], wo[0, :, cols]) + dot(a_all[rows, 256:512], wo[1, :, cols])

    pltpu.make_async_remote_copy(
        fv_all.at[1 - r], fv_all.at[1 - r], sp.at[2], rp.at[2], partner, MESH
    ).wait_recv()
    pltpu.make_async_remote_copy(
        wo.at[1 - r], wo.at[1 - r], sp.at[0], rp.at[0], partner, MESH
    ).wait_recv()
    attend(0)
    heads_out(slice(0, 32))
    for c in range(CHUNKS):
        send_c[c, 0] = projected(slice(0, 32), c).astype(BF16)
        copy_c(c, 0).start()
    for p in range(1, 4):
        attend(p)
    heads_out(slice(32, 128))
    for c in range(CHUNKS):
        part = projected(slice(32, 128), c)
        send_c[c, 1] = part[0:32].astype(BF16)
        acc[c] = part[32:96].reshape(2, 32, width)
        copy_c(c, 1).start()

    own_lat = lat_q[96:128, :]
    own_patch = pl.multiple_of(((m % 2) * 2 + r) * 32, 32)
    for c in range(CHUNKS):
        cols = slice(width * c, width * c + width)
        embedded = dot(own_lat, e[:, cols]) + pos[pl.ds(own_patch, 32), cols].astype(F32)
        acc[c, 1] = acc[c, 1] + embedded
    for c in range(CHUNKS):
        land_c(c, 0).wait_recv()
        send_c[c, 2] = (acc[c, 0] + recv_c[c, 0].astype(F32)).astype(BF16)
        copy_c(c, 2).start()
    outs = []
    for c in range(CHUNKS):
        cols = slice(width * c, width * c + width)
        total = acc[c, 1]
        for p in (1, 2):
            land_c(c, p).wait_recv()
            total = total + recv_c[c, p].astype(F32)
        out_ref[:, cols] = total.astype(BF16)
        outs.append(
            pltpu.make_async_copy(out_ref.at[:, cols], out_hbm.at[:, cols], out_sem.at[c])
        )
        outs[-1].start()

    for step in range(1, 8):
        copy_a(step).wait_send()
        copy_x(step).wait_send()
        copy_z(step).wait_send()

    @pl.when(jnp.logical_not(is_self))
    def _():
        copy_z(0).wait_send()

    for idx in range(8):
        forward(idx).wait_send()
    wo_copy.wait_send()
    m_copy.wait_send()
    f_copy.wait_send()
    for c in range(CHUNKS):
        for p in range(3):
            copy_c(c, p).wait_send()
    for copy in outs:
        copy.wait()


def on_device(
    gen_hidden,
    gen_out_weight,
    patch_order,
    frame_block,
    embed_weight,
    pos_table,
    norm_gain,
    qkv_weight,
    out_weight,
):
    any_space = pl.BlockSpec(memory_space=pl.ANY)
    dma = pltpu.SemaphoreType.DMA
    width = 3072 // CHUNKS
    scratch = [
        pltpu.VMEM((256, 384), BF16),
        pltpu.VMEM((384, 128), BF16),
        pltpu.VMEM((1, 128), jnp.int32),
        pltpu.SMEM((256,), jnp.int32),
        pltpu.VMEM((24, 128), BF16),
        pltpu.VMEM((32, 3072), BF16),
        pltpu.VMEM((128, 3072), BF16),
        pltpu.VMEM((128, 3072), BF16),
        pltpu.VMEM((3, 3072, 256), BF16),
        pltpu.VMEM((2, 256, 3072), BF16),
        pltpu.VMEM((288, 128), F32),
        pltpu.VMEM((8, 48, 128), F32),
        pltpu.VMEM((8, 48, 128), BF16),
        pltpu.VMEM((8, 48, 128), BF16),
        pltpu.VMEM((8, 16, 128), BF16),
        pltpu.VMEM((8, 16, 128), BF16),
        pltpu.VMEM((2, 64, 128), BF16),
        pltpu.VMEM((2, 2, 8, 64, 128), BF16),
        pltpu.VMEM((2, 1024, 256), BF16),
        pltpu.VMEM((512, 3072), BF16),
        pltpu.VMEM((2, 2, 256, 512), BF16),
        pltpu.VMEM((2, 2, 256, 256), BF16),
        pltpu.VMEM((4, 32, 1024), BF16),
        pltpu.VMEM((1024, 128), F32),
        pltpu.VMEM((128, 128), F32),
        pltpu.VMEM((128, 128), F32),
        pltpu.VMEM((4, 1, 256), F32),
        pltpu.VMEM((2, 2, 1, 1024), F32),
        pltpu.VMEM((2, 4, 1, 256), F32),
        pltpu.VMEM((128, 256), BF16),
        pltpu.VMEM((128, 128), BF16),
        pltpu.VMEM((4, 128, 256), BF16),
        pltpu.VMEM((4, 128, 256), F32),
        pltpu.VMEM((128, 512), BF16),
        pltpu.VMEM((CHUNKS, 2, 32, width), F32),
        pltpu.VMEM((CHUNKS, 3, 32, width), BF16),
        pltpu.VMEM((CHUNKS, 3, 32, width), BF16),
        pltpu.SemaphoreType.REGULAR((8,)),
        pltpu.SemaphoreType.REGULAR,
        dma((9,)),
        dma((CHUNKS,)),
        dma((8,)),
        dma((8,)),
        dma((8,)),
        dma((8,)),
        dma((8,)),
        dma((8,)),
        dma((8,)),
        dma((8,)),
        dma((3,)),
        dma((3,)),
        dma((CHUNKS, 3)),
        dma((CHUNKS, 3)),
    ]
    return pl.pallas_call(
        kernel,
        out_shape=jax.ShapeDtypeStruct((32, 3072), BF16),
        in_specs=[any_space] * 9,
        out_specs=any_space,
        scratch_shapes=scratch,
        compiler_params=pltpu.CompilerParams(collective_id=0, has_side_effects=True),
    )(
        gen_hidden.reshape(256, 384),
        gen_out_weight,
        patch_order.reshape(1, 128),
        frame_block,
        embed_weight,
        pos_table,
        norm_gain.reshape(24, 128),
        jnp.transpose(qkv_weight, (1, 0, 2)),
        out_weight,
    )


def solution(mesh):
    in_specs = (
        P("seq", None, ("mp", "role")),
        P(("mp", "role"), None),
        P(),
        P(),
        P(),
        P(),
        P(),
        P(None, None, ("mp", "role")),
        P(("mp", "role"), None),
    )
    out_specs = P(("seq", "mp", "role"), None)
    return jax.shard_map(
        on_device, mesh=mesh, in_specs=in_specs, out_specs=out_specs, check_vma=False
    )
```

```python
import functools

import jax
import jax.numpy as jnp
from jax import lax
from jax.experimental import pallas as pl
from jax.experimental.pallas import tpu as pltpu
from jax.sharding import PartitionSpec as P

MESH = pl.DeviceIdType.MESH
F32 = jnp.float32
BF16 = jnp.bfloat16
HS = 128
CHUNKS = 6
FAR_FIRST = (4, 3, 5, 2, 6, 1, 7)
NEG = -1e30


def dot(a, b, precision=None):
    return jnp.dot(a, b, preferred_element_type=F32, precision=precision)


def dot_t(a, b, precision=None):
    return lax.dot_general(
        a, b, (((1,), (1,)), ((), ())), preferred_element_type=F32, precision=precision
    )


def split2(a):
    hi = a.astype(BF16)
    return hi, (a - hi.astype(F32)).astype(BF16)


def iota(shape, dim):
    return lax.broadcasted_iota(jnp.int32, shape, dim)


def slot_of(row):
    part = lax.shift_right_logical(row, 3)
    parity = lax.shift_right_logical(part, 6)
    half = jnp.bitwise_and(lax.shift_right_logical(part, 5), 1)
    rest = jnp.bitwise_and(lax.shift_right_logical(part, 3), 3)
    return half * 64 + rest * 16 + parity * 8 + jnp.bitwise_and(part, 7)


def kernel(
    gh_hbm,
    gw_hbm,
    po_hbm,
    fb_hbm,
    e_hbm,
    pos_hbm,
    gain_hbm,
    w_hbm,
    wo_hbm,
    out_hbm,
    gh,
    gw,
    po_ref,
    fb_ref,
    gain_ref,
    out_ref,
    e,
    pos,
    w,
    wo,
    ppad,
    mine,
    send_a,
    recv_a,
    send_x,
    recv_x,
    send_z,
    lat,
    kv,
    fhl,
    m_all,
    fv_all,
    sel_q,
    hr2,
    he2,
    ncol,
    nlane,
    bias,
    key_scale,
    gg,
    lat_q,
    q_all,
    u_all,
    a_all,
    acc,
    send_c,
    recv_c,
    entered,
    allowed,
    load_sem,
    out_sem,
    sa,
    ra,
    sx,
    rx,
    sz,
    rz,
    sf,
    rf,
    sp,
    rp,
    sc,
    rc,
):
    seq = lax.axis_index("seq")
    m = lax.axis_index("mp")
    r = lax.axis_index("role")
    ys = seq // 64
    z = (seq // 8) % 8
    x = seq % 8
    j = 2 * m + r
    y = ys * 4 + m
    is_self = jnp.logical_and(j == z, True)

    def group(k):
        return (seq, k // 2, k % 2)

    def row_x(x2):
        return (ys * 64 + z * 8 + x2, m, r)

    def ring(y2, role):
        return ((y2 // 4) * 64 + z * 8 + x, y2 % 4, role)

    def row_z(z2):
        return (ys * 64 + z2 * 8 + x, m, r)

    def zy_dest(i):
        y2 = (y + i) % 8
        return ((y2 // 4) * 64 + j * 8 + x, y2 % 4, z % 2)

    side = 1 - 2 * r
    offsets = (2, -1, 1, 0)

    def place_of(p):
        return (y + side * offsets[p] + 8) % 8

    partner = (seq, m, 1 - r)

    def load(src, dst, n):
        return pltpu.make_async_copy(src, dst, load_sem.at[n])

    load_gh = load(gh_hbm, gh, 0)
    load_gw = load(gw_hbm, gw, 1)
    load_po = load(po_hbm, po_ref, 2)
    load_fb = load(fb_hbm, fb_ref, 3)
    load_gain = load(gain_hbm, gain_ref, 4)
    load_e = load(e_hbm, e, 5)
    load_pos = load(pos_hbm, pos, 6)
    load_w = load(w_hbm, w, 7)
    load_wo = load(wo_hbm, wo.at[r], 8)
    load_gh.start()
    load_gw.start()

    barrier = pltpu.get_barrier_semaphore()

    def greet(device):
        pl.semaphore_signal(barrier, inc=1, device_id=device, device_id_type=MESH)

    for step in FAR_FIRST:
        greet(row_z((z + step) % 8))
        greet(row_x((x + step) % 8))
        greet(ring((y + step) % 8, r))
        greet(ring((y + step) % 8, 1 - r))
    greet(partner)

    for copy in (load_po, load_fb, load_gain):
        copy.start()
    ppad[0:8, :] = jnp.zeros((8, 128), F32)
    ppad[264:288, :] = jnp.zeros((24, 128), F32)

    load_gh.wait()
    load_gw.wait()
    ppad[8:264, :] = dot(gh[...], gw[...])
    for k in range(8):
        parts = [ppad[128 * yt + 16 * k + 5 : 128 * yt + 16 * k + 29, :] for yt in range(2)]
        part = jnp.concatenate(parts, axis=0)
        mine[k] = part
        send_a[k] = part.astype(BF16)

    pl.semaphore_wait(barrier, 29)

    def copy_a(step):
        k = (j + step) % 8
        return pltpu.make_async_remote_copy(
            send_a.at[k], recv_a.at[j], sa.at[step], ra.at[j], group(k), MESH
        )

    def land_a(step):
        k = (j + step) % 8
        return pltpu.make_async_remote_copy(
            send_a.at[k], recv_a.at[k], sa.at[step], ra.at[k], group(k), MESH
        )

    for step in range(1, 8):
        copy_a(step).start()
    for z2 in range(8):

        @pl.when(jnp.logical_and(z2 != z, r == z2 % 2))
        def _():
            pl.semaphore_signal(entered.at[z], inc=1, device_id=row_z(z2), device_id_type=MESH)

    for copy in (load_e, load_pos, load_w, load_wo):
        copy.start()
    wo_copy = pltpu.make_async_remote_copy(
        wo_hbm, wo.at[r], sp.at[0], rp.at[0], partner, MESH
    )
    wo_copy.start()

    load_po.wait()
    load_fb.wait()
    po_f = jnp.broadcast_to(po_ref[...], (16, 128)).astype(F32).astype(BF16)
    spread = (iota((128, 1024), 0) == slot_of(iota((128, 1024), 1))).astype(F32).astype(BF16)
    po_lane = dot(po_f, spread)[0:1]
    perm_t = (jnp.broadcast_to(po_ref[...], (128, 128)) == iota((128, 128), 0)).astype(F32).astype(
        BF16
    )
    rows8 = (slot_of(iota((1024, 128), 0)) == iota((1024, 128), 1)).astype(F32).astype(BF16)
    onehot = dot_t(rows8, perm_t).astype(BF16)
    kv[0, :, 128:256] = onehot
    kv[1, :, 128:256] = onehot
    w_lane = jnp.bitwise_and(iota((1, 1024), 1), 7)
    for yt in range(2):
        base = yt * 128 + z * 16 + x * 2 - 3
        blocks = []
        key_block = jnp.full((1, 1024), -1, jnp.int32)
        for n in range(8):
            frame = base + n
            value = fb_ref[jnp.clip(frame, 0, 255)]
            value = jnp.where(jnp.logical_and(frame >= 0, frame <= 255), value, -1)
            blocks.append(value)
            key_block = jnp.where(w_lane == n, value, key_block)
        for fi in range(2):
            bias[yt, fi] = jnp.where(key_block == blocks[3 + fi], F32(0), F32(NEG))
    for p in range(4):
        d = place_of(p)
        fi = (d % 4) // 2
        patch = ((d % 2) * 2 + r) * 32
        rows = (iota((32, 1024), 0) + patch).astype(F32)
        hit = jnp.logical_and(
            jnp.broadcast_to(po_lane, (32, 1024)) == rows,
            jnp.broadcast_to(w_lane, (32, 1024)) == 3 + fi,
        )
        sel_q[p] = hit.astype(F32).astype(BF16)

    def weight_product(c):
        both = dot(fhl[...], w[c])
        return both[0:256] + both[256:512]

    for step in range(1, 8):
        land_a(step).wait_recv()
    @pl.when(r == z % 2)
    def _():
        for z2 in range(8):

            @pl.when(z2 != z)
            def _():
                pl.semaphore_wait(entered.at[z2], 1)

            for half_y in range(2):

                @pl.when(jnp.logical_not(jnp.logical_and(ys == half_y, j == z2)))
                def _():
                    pl.semaphore_signal(
                        allowed,
                        inc=1,
                        device_id=(half_y * 64 + z * 8 + x, z2 // 2, z2 % 2),
                        device_id_type=MESH,
                    )

    total = mine[j]
    for step in range(1, 8):
        total = total + recv_a[(j + step) % 8].astype(F32)
    mine[j] = total
    for n in range(8):
        halves = [mine[j, 24 * yt + 2 * n : 24 * yt + 2 * n + 8, :] for yt in range(2)]
        send_x[n] = jnp.concatenate(halves, axis=0).astype(BF16)

    def copy_x(step):
        x2 = (x + step) % 8
        return pltpu.make_async_remote_copy(
            send_x.at[x2], recv_x.at[x], sx.at[step], rx.at[x], row_x(x2), MESH
        )

    def land_x(step):
        x2 = (x + step) % 8
        return pltpu.make_async_remote_copy(
            send_x.at[x2], recv_x.at[x2], sx.at[step], rx.at[x2], row_x(x2), MESH
        )

    for step in FAR_FIRST:
        copy_x(step).start()
    recv_x[x] = send_x[x]

    load_e.wait()
    load_pos.wait()
    load_gain.wait()
    gain = gain_ref[...].astype(F32)
    for n, table in enumerate((e, pos)):
        for part in range(24):
            cols = slice(128 * part, 128 * part + 128)
            hi, lo = split2(table[:, cols].astype(F32) * gain[part : part + 1, :])
            fhl[n * 128 : n * 128 + 128, cols] = hi
            fhl[256 + n * 128 : 384 + n * 128, cols] = lo
    ghi, glo = split2(dot_t(e[...], e[...]))
    gg[:, 0:128] = ghi
    gg[:, 128:256] = glo
    he = 2.0 * dot_t(pos[...], e[...])
    he2[...] = he
    he_hi, he_lo = split2(he)
    hr2[...] = dot(onehot, he_hi) + dot(onehot, he_lo)
    norms = dot_t(pos[...], pos[...])
    diagonal = jnp.where(iota((128, 128), 0) == iota((128, 128), 1), norms, F32(0))
    ncol[...] = jnp.broadcast_to(jnp.sum(diagonal, axis=1, keepdims=True), (128, 128))
    nrow = jnp.broadcast_to(jnp.sum(diagonal, axis=0, keepdims=True), (8, 128))
    norm_lane = dot_t(nrow, onehot.astype(F32), lax.Precision.HIGHEST)[0:1]
    for n in range(4):
        nlane[n] = norm_lane[:, 256 * n : 256 * n + 256]
    load_w.wait()
    load_wo.wait()

    for step in range(1, 8):
        land_x(step).wait_recv()
    for a in range(4):
        first = recv_x[2 * a].astype(F32)
        second = recv_x[2 * a + 1].astype(F32)
        for yt in range(2):
            pair = jnp.concatenate(
                [first[8 * yt : 8 * yt + 8], second[8 * yt : 8 * yt + 8]], axis=0
            )
            send_z[yt, 16 * a : 16 * a + 16, :] = pair.astype(BF16)

    half = z % 2
    own_idx = ys * 4 + z // 2

    def copy_z(i):
        return pltpu.make_async_remote_copy(
            send_z, lat.at[:, half, own_idx], sz.at[i], rz.at[own_idx], zy_dest(i), MESH
        )

    local_z = pltpu.make_async_copy(send_z, lat.at[:, half, own_idx], rz.at[own_idx])
    pl.semaphore_wait(allowed, 8 - (r == z % 2).astype(jnp.int32))
    for i in FAR_FIRST:
        copy_z(i).start()

    @pl.when(jnp.logical_not(is_self))
    def _():
        copy_z(0).start()

    @pl.when(is_self)
    def _():
        local_z.start()

    fq = weight_product(0)
    fk = weight_product(1)
    for h in range(2):
        cols = slice(HS * h, HS * h + HS)
        bil = dot_t(fq[:, cols], fk[:, cols], lax.Precision.HIGHEST)
        hi, lo = split2(bil)
        m_all[r, 0, :, 256 * h : 256 * h + 256] = hi
        m_all[r, 1, :, 256 * h : 256 * h + 256] = lo
    hi, lo = split2(weight_product(2))
    fv_all[r, 0] = hi
    fv_all[r, 1] = lo
    m_copy = pltpu.make_async_remote_copy(
        m_all.at[r], m_all.at[r], sp.at[1], rp.at[1], partner, MESH
    )
    f_copy = pltpu.make_async_remote_copy(
        fv_all.at[r], fv_all.at[r], sp.at[2], rp.at[2], partner, MESH
    )
    m_copy.start()
    f_copy.start()

    def forward(idx):
        block = lat.at[:, r, idx]
        return pltpu.make_async_remote_copy(
            block, block, sf.at[idx], rf.at[idx], partner, MESH
        )

    def forwarded(idx):
        block = lat.at[:, 1 - r, idx]
        return pltpu.make_async_remote_copy(
            block, block, sf.at[idx], rf.at[idx], partner, MESH
        )

    ones = jnp.ones((16, 128), F32).astype(BF16)

    def take_batch(parity, n):
        batch = parity * 2 + n
        first = pl.multiple_of(batch * 256, 256)
        for yt in range(2):
            rows = lat[yt, parity, 4 * n : 4 * n + 4].reshape(256, 128)
            kv[yt, pl.ds(first, 256), 0:128] = rows
            both = dot(rows, gg[...])
            cross = both[:, 0:128] + both[:, 128:256] + hr2[pl.ds(first, 256), :]
            hi, lo = split2(rows.astype(F32) * cross)
            total = dot_t(ones, hi)[0:1] + dot_t(ones, lo)[0:1] + nlane[batch]
            key_scale[yt, batch] = lax.rsqrt(
                jnp.maximum(total, 0.0) * F32(1 / 3072) + F32(1e-06)
            )

    for n in range(2):
        for idx in range(4 * n, 4 * n + 4):
            block = lat.at[:, r, idx]
            pltpu.make_async_copy(block, block, rz.at[idx]).wait()
            forward(idx).start()
        take_batch(r, n)
        for idx in range(4 * n, 4 * n + 4):
            forwarded(idx).wait_recv()
        take_batch(1 - r, n)

    tokens = []
    scales = []
    for p in range(4):
        d = place_of(p)
        patch = pl.multiple_of(((d % 2) * 2 + r) * 32, 32)
        chosen = dot(sel_q[p], kv[d // 4, :, 0:128])
        lat_q[32 * p : 32 * p + 32, :] = chosen.astype(BF16)
        both = dot(chosen.astype(BF16), gg[...])
        squares = chosen * (both[:, 0:128] + both[:, 128:256] + he2[pl.ds(patch, 32), :])
        total = jnp.sum(squares, axis=1, keepdims=True) + ncol[pl.ds(patch, 32), 0:1]
        scales.append(
            lax.rsqrt(jnp.maximum(total, 0.0) * F32(1 / 3072) + F32(1e-06))
            * F32(1 / HS**0.5)
        )
        place = (iota((32, 128), 0) + patch == iota((32, 128), 1)).astype(F32).astype(BF16)
        tokens.append(jnp.concatenate([chosen.astype(BF16), place], axis=1))
    tokens = jnp.concatenate(tokens, axis=0)
    scales = jnp.concatenate(scales, axis=0)
    pltpu.make_async_remote_copy(
        m_all.at[1 - r], m_all.at[1 - r], sp.at[1], rp.at[1], partner, MESH
    ).wait_recv()
    for role in range(2):
        q = (dot(tokens, m_all[role, 0]) + dot(tokens, m_all[role, 1])) * scales
        for h in range(2):
            q_all[2 * role + h] = q[:, 256 * h : 256 * h + 256].astype(BF16)

    width = 3072 // CHUNKS

    def copy_c(c, p):
        step = -side if p == 1 else side
        return pltpu.make_async_remote_copy(
            send_c.at[c, p],
            recv_c.at[c, p],
            sc.at[c, p],
            rc.at[c, p],
            ring((y + step + 8) % 8, r),
            MESH,
        )

    def land_c(c, p):
        step = side if p == 1 else -side
        return pltpu.make_async_remote_copy(
            send_c.at[c, p],
            recv_c.at[c, p],
            sc.at[c, p],
            rc.at[c, p],
            ring((y + step + 8) % 8, r),
            MESH,
        )

    def attend(p):
        d = place_of(p)
        yt = d // 4
        fi = (d % 4) // 2
        keys = kv[yt]
        q = q_all[:, 32 * p : 32 * p + 32, :].reshape(128, 256)
        scale = jnp.concatenate([key_scale[yt, n] for n in range(4)], axis=1)
        s = dot_t(q, keys) * scale + bias[yt, fi]
        top = jnp.max(s, axis=1, keepdims=True)
        expo = jnp.exp(s - top)
        norm = jnp.sum(expo, axis=1, keepdims=True)
        u = dot((expo * scale).astype(BF16), keys) / norm
        u_all[:, 32 * p : 32 * p + 32, :] = u.reshape(4, 32, 256)

    def heads_out(rows):
        for role in range(2):
            for h in range(2):
                hi, lo = split2(u_all[2 * role + h, rows, :])
                cols = slice(HS * h, HS * h + HS)
                v_hi = fv_all[role, 0, :, cols]
                v_lo = fv_all[role, 1, :, cols]
                a = dot(hi, v_hi) + dot(lo, v_hi) + dot(hi, v_lo)
                a_all[rows, 256 * role + HS * h : 256 * role + HS * h + HS] = a.astype(BF16)

    def projected(rows, c):
        cols = slice(width * c, width * c + width)
        return dot(a_all[rows, 0:256], wo[0, :, cols]) + dot(a_all[rows, 256:512], wo[1, :, cols])

    pltpu.make_async_remote_copy(
        fv_all.at[1 - r], fv_all.at[1 - r], sp.at[2], rp.at[2], partner, MESH
    ).wait_recv()
    pltpu.make_async_remote_copy(
        wo.at[1 - r], wo.at[1 - r], sp.at[0], rp.at[0], partner, MESH
    ).wait_recv()
    attend(0)
    heads_out(slice(0, 32))
    for c in range(CHUNKS):
        send_c[c, 0] = projected(slice(0, 32), c).astype(BF16)
        copy_c(c, 0).start()
    for p in range(1, 4):
        attend(p)
    heads_out(slice(32, 128))
    for c in range(CHUNKS):
        part = projected(slice(32, 128), c)
        send_c[c, 1] = part[0:32].astype(BF16)
        acc[c] = part[32:96].reshape(2, 32, width)
        copy_c(c, 1).start()

    own_lat = lat_q[96:128, :]
    own_patch = pl.multiple_of(((m % 2) * 2 + r) * 32, 32)
    for c in range(CHUNKS):
        cols = slice(width * c, width * c + width)
        embedded = dot(own_lat, e[:, cols]) + pos[pl.ds(own_patch, 32), cols].astype(F32)
        acc[c, 1] = acc[c, 1] + embedded
    for c in range(CHUNKS):
        land_c(c, 0).wait_recv()
        send_c[c, 2] = (acc[c, 0] + recv_c[c, 0].astype(F32)).astype(BF16)
        copy_c(c, 2).start()
    outs = []
    for c in range(CHUNKS):
        cols = slice(width * c, width * c + width)
        total = acc[c, 1]
        for p in (1, 2):
            land_c(c, p).wait_recv()
            total = total + recv_c[c, p].astype(F32)
        out_ref[:, cols] = total.astype(BF16)
        outs.append(
            pltpu.make_async_copy(out_ref.at[:, cols], out_hbm.at[:, cols], out_sem.at[c])
        )
        outs[-1].start()

    for step in range(1, 8):
        copy_a(step).wait_send()
        copy_x(step).wait_send()
        copy_z(step).wait_send()

    @pl.when(jnp.logical_not(is_self))
    def _():
        copy_z(0).wait_send()

    for idx in range(8):
        forward(idx).wait_send()
    wo_copy.wait_send()
    m_copy.wait_send()
    f_copy.wait_send()
    for c in range(CHUNKS):
        for p in range(3):
            copy_c(c, p).wait_send()
    for copy in outs:
        copy.wait()


def on_device(
    gen_hidden,
    gen_out_weight,
    patch_order,
    frame_block,
    embed_weight,
    pos_table,
    norm_gain,
    qkv_weight,
    out_weight,
):
    any_space = pl.BlockSpec(memory_space=pl.ANY)
    dma = pltpu.SemaphoreType.DMA
    width = 3072 // CHUNKS
    scratch = [
        pltpu.VMEM((256, 384), BF16),
        pltpu.VMEM((384, 128), BF16),
        pltpu.VMEM((1, 128), jnp.int32),
        pltpu.SMEM((256,), jnp.int32),
        pltpu.VMEM((24, 128), BF16),
        pltpu.VMEM((32, 3072), BF16),
        pltpu.VMEM((128, 3072), BF16),
        pltpu.VMEM((128, 3072), BF16),
        pltpu.VMEM((3, 3072, 256), BF16),
        pltpu.VMEM((2, 256, 3072), BF16),
        pltpu.VMEM((288, 128), F32),
        pltpu.VMEM((8, 48, 128), F32),
        pltpu.VMEM((8, 48, 128), BF16),
        pltpu.VMEM((8, 48, 128), BF16),
        pltpu.VMEM((8, 16, 128), BF16),
        pltpu.VMEM((8, 16, 128), BF16),
        pltpu.VMEM((2, 64, 128), BF16),
        pltpu.VMEM((2, 2, 8, 64, 128), BF16),
        pltpu.VMEM((2, 1024, 256), BF16),
        pltpu.VMEM((512, 3072), BF16),
        pltpu.VMEM((2, 2, 256, 512), BF16),
        pltpu.VMEM((2, 2, 256, 256), BF16),
        pltpu.VMEM((4, 32, 1024), BF16),
        pltpu.VMEM((1024, 128), F32),
        pltpu.VMEM((128, 128), F32),
        pltpu.VMEM((128, 128), F32),
        pltpu.VMEM((4, 1, 256), F32),
        pltpu.VMEM((2, 2, 1, 1024), F32),
        pltpu.VMEM((2, 4, 1, 256), F32),
        pltpu.VMEM((128, 256), BF16),
        pltpu.VMEM((128, 128), BF16),
        pltpu.VMEM((4, 128, 256), BF16),
        pltpu.VMEM((4, 128, 256), F32),
        pltpu.VMEM((128, 512), BF16),
        pltpu.VMEM((CHUNKS, 2, 32, width), F32),
        pltpu.VMEM((CHUNKS, 3, 32, width), BF16),
        pltpu.VMEM((CHUNKS, 3, 32, width), BF16),
        pltpu.SemaphoreType.REGULAR((8,)),
        pltpu.SemaphoreType.REGULAR,
        dma((9,)),
        dma((CHUNKS,)),
        dma((8,)),
        dma((8,)),
        dma((8,)),
        dma((8,)),
        dma((8,)),
        dma((8,)),
        dma((8,)),
        dma((8,)),
        dma((3,)),
        dma((3,)),
        dma((CHUNKS, 3)),
        dma((CHUNKS, 3)),
    ]
    return pl.pallas_call(
        kernel,
        out_shape=jax.ShapeDtypeStruct((32, 3072), BF16),
        in_specs=[any_space] * 9,
        out_specs=any_space,
        scratch_shapes=scratch,
        compiler_params=pltpu.CompilerParams(collective_id=0, has_side_effects=True),
    )(
        gen_hidden.reshape(256, 384),
        gen_out_weight,
        patch_order.reshape(1, 128),
        frame_block,
        embed_weight,
        pos_table,
        norm_gain.reshape(24, 128),
        jnp.transpose(qkv_weight, (1, 0, 2)),
        out_weight,
    )


def solution(mesh):
    in_specs = (
        P("seq", None, ("mp", "role")),
        P(("mp", "role"), None),
        P(),
        P(),
        P(),
        P(),
        P(),
        P(None, None, ("mp", "role")),
        P(("mp", "role"), None),
    )
    out_specs = P(("seq", "mp", "role"), None)
    return jax.shard_map(
        on_device, mesh=mesh, in_specs=in_specs, out_specs=out_specs, check_vma=False
    )
```
